128 devices in a mesh: rows: 4 (over x), cols: 32 (over y, z, core).
Axes of the slice: x: 4, y: 4, z: 4, core: 2. Of those that a mesh axis runs over, the one named last changes fastest.
Arguments:
- left_image: bfloat16 [128, 8192], P(('rows', 'cols')), may hold values from -8 to 8, as said below
- right_image: bfloat16 [128, 8192], P(('rows', 'cols')), may hold values from -8 to 8, as said below
- ranges: int32 [32, 2], replicated, may hold values from 0 to 63, as said below
Outputs:
- best_score: float32 [128, 8192], P('rows', 'cols')
The draws below stay inside these ranges and needn't reach their ends.
Inputs may be any that keep to these rules, and one draw needn't show every extreme that they name: `left_image`: pixel values. `right_image`: pixel values. `ranges`: row t holds tile t's first disparity (column 0, 0 to 63) and its number of blocks of 128 disparities (column 1, 1 to 2); some tile has 2 blocks, some tile starts at 0 and some at 63.
All inputs are finite; a program needn't handle non-finite values.
Results may differ from the reference program's by a relative error of at most 0.0003.
Values may be sent and summed in bfloat16 or wider, within the bound.
A program may use at most 128 MiB of HBM per device.

```python
import math
import jax
import jax.numpy as jnp
from jax import lax

TW = 256
DB = 128
MAXB = 2
SMAX = 64
TILES = 32
H = 128
W = 8192


def texture(key):
    amp_key, noise_key = jax.random.split(jax.random.fold_in(key, 11))
    levels = jnp.exp(jax.random.uniform(amp_key, (H // 8, W // 8), jnp.float32, math.log(0.03), math.log(1.0)))
    grain = jnp.clip(jax.random.normal(noise_key, (H, W), jnp.float32), -4.0, 4.0)
    scale = jnp.repeat(jnp.repeat(levels, 8, axis=0), 8, axis=1)
    return (scale * grain, scale)


def draw_left_image(key, part):
    pattern, scale = texture(key)
    return pattern.astype(jnp.bfloat16)


def draw_right_image(key, part):
    pattern, scale = texture(key)
    shifts = jax.random.randint(jax.random.fold_in(key, 13), (H // 8,), 0, SMAX + DB * MAXB, jnp.int32)
    per_row = jnp.repeat(shifts, 8)
    columns = jnp.arange(W, dtype=jnp.int32)[None, :] + per_row[:, None]
    inside = columns < W
    moved = jnp.take_along_axis(pattern, jnp.minimum(columns, W - 1), axis=1)
    moved = jnp.where(inside, moved, 0.0)
    grain = jnp.clip(jax.random.normal(jax.random.fold_in(key, 17), (H, W), jnp.float32), -4.0, 4.0)
    return (0.8 * moved + 0.4 * scale * grain).astype(jnp.bfloat16)


def draw_ranges(key, part):
    first_key, count_key, pick_key = jax.random.split(jax.random.fold_in(key, 19), 3)
    starts = jax.random.randint(first_key, (TILES,), 0, SMAX, jnp.int32)
    counts = jax.random.randint(count_key, (TILES,), 1, MAXB + 1, jnp.int32)
    heavy = jax.random.randint(pick_key, (), 0, TILES, jnp.int32)
    tile_ids = jnp.arange(TILES, dtype=jnp.int32)
    counts = jnp.where(tile_ids == heavy, MAXB, counts)
    starts = jnp.where(tile_ids == heavy, 0, starts)
    starts = jnp.where(tile_ids == (heavy + 1) % TILES, SMAX - 1, starts)
    return jnp.stack([starts, counts], axis=1)


def setup_inputs(seed: int = 0) -> dict:
    splits = jax.random.split(jax.random.key(seed), 4)
    return {
        "left_image": draw_left_image(jax.random.fold_in(splits[3], 71), 0),
        "right_image": draw_right_image(jax.random.fold_in(splits[3], 71), 0),
        "ranges": draw_ranges(jax.random.fold_in(splits[3], 71), 0),
    }


def box_sum(values, along):
    length = values.shape[along] - 6
    running = lax.slice_in_dim(values, 0, length, axis=along)
    for offset in range(1, 7):
        running = running + lax.slice_in_dim(values, offset, offset + length, axis=along)
    return running

def window_sums(values):
    return box_sum(box_sum(values, values.ndim - 1), values.ndim - 2)

def moments(pixels):
    average = window_sums(pixels) / 49.0
    spread = jnp.maximum(window_sums(pixels * pixels) / 49.0 - average * average, 0.01)
    return (average, spread)

def skewed(values, columns, lanes):
    lead = values.shape[:-1]
    length = values.shape[-1]
    tiled = jnp.broadcast_to(values[..., None, :], lead + (lanes + 1, length))
    flat = tiled.reshape(lead + ((lanes + 1) * length,))
    sheared = flat[..., :lanes * (length + 1)].reshape(lead + (lanes, length + 1))
    sheared = jnp.flip(sheared[..., :columns], axis=-2)
    return jnp.swapaxes(sheared, -1, -2)

def best_scores(left_pad, right_pad, block_count):
    height = left_pad.shape[0] - 6
    tile_width = left_pad.shape[1] - 6
    left_mean, left_spread = moments(left_pad)
    right_mean, right_spread = moments(right_pad)
    right_stats = jnp.stack([right_mean, right_spread])
    col_block = 256 if tile_width % 256 == 0 else 128
    col_blocks = tile_width // col_block

    def visitor(step_index, current):
        block_id = step_index // col_blocks
        col_start = step_index % col_blocks * col_block
        source_at = col_start + 61 + DB * (MAXB - block_id) - (DB - 1)
        right_cut = lax.dynamic_slice_in_dim(right_pad, source_at, col_block + 6 + DB - 1, 1)
        right_lanes = skewed(right_cut, col_block + 6, DB)
        left_cut = lax.dynamic_slice_in_dim(left_pad, col_start, col_block + 6, 1)
        product = left_cut[:, :, None] * right_lanes
        cross_term = box_sum(box_sum(product, 1), 0) / 49.0
        stats_cut = lax.dynamic_slice_in_dim(right_stats, source_at, col_block + DB - 1, 2)
        stats_lanes = skewed(stats_cut, col_block, DB)
        mean_l = lax.dynamic_slice_in_dim(left_mean, col_start, col_block, 1)[:, :, None]
        spread_l = lax.dynamic_slice_in_dim(left_spread, col_start, col_block, 1)[:, :, None]
        scores = (cross_term - mean_l * stats_lanes[0]) / jnp.sqrt(spread_l * stats_lanes[1])
        best = lax.optimization_barrier(jnp.max(scores, axis=-1))
        old = lax.dynamic_slice_in_dim(current, col_start, col_block, 1)
        return lax.dynamic_update_slice_in_dim(current, jnp.maximum(old, best), col_start, 1)
    initial = jnp.full((height, tile_width), -2.0, jnp.float32)
    return lax.fori_loop(0, block_count * col_blocks, visitor, initial)

def reference(left_image, right_image, ranges):
    lead_pad = SMAX + DB * MAXB + 64
    window_width = TW + DB * (MAXB + 1)
    left_full = jnp.pad(left_image.astype(jnp.float32), 3)
    right_full = jnp.pad(right_image.astype(jnp.float32), ((3, 3), (lead_pad, 64)))

    def per_tile(tile_id):
        left_pad = lax.dynamic_slice_in_dim(left_full, tile_id * TW, TW + 6, 1)
        window_at = tile_id * TW - ranges[tile_id, 0] + SMAX
        right_pad = lax.dynamic_slice_in_dim(right_full, window_at, window_width, 1)
        return best_scores(left_pad, right_pad, ranges[tile_id, 1])
    tiles_out = lax.map(per_tile, jnp.arange(TILES, dtype=jnp.int32))
    return jnp.transpose(tiles_out, (1, 0, 2)).reshape(H, W)
```

```python
import jax
import jax.numpy as jnp
from jax import lax
from jax.experimental import pallas as pl
from jax.experimental.pallas import tpu as pltpu
from jax.sharding import PartitionSpec as P

F32, BF16 = jnp.float32, jnp.bfloat16

def split3(x):
    hi = x.astype(BF16)
    r = x - hi.astype(F32)
    mid = r.astype(BF16)
    lo = (r - mid.astype(F32)).astype(BF16)
    return hi, mid, lo

def box_rows(h):
    out = h[0:32]
    for i in range(1, 7):
        out = out + h[i:i + 32]
    return out

def stats(shifted):
    h = shifted[0]
    q = shifted[0] * shifted[0]
    for v in shifted[1:]:
        h = h + v
        q = q + v * v
    total = box_rows(h)
    mean = total * (1.0 / 49.0)
    spread = jnp.maximum(box_rows(q) * (1.0 / 49.0) - mean * mean, 0.01)
    return total, mean, lax.rsqrt(spread)

def compute(L, R, s, two, out_ref, acc_ref):
    Ls = pltpu.roll(L, 768 - 381, 1)
    Lj = [Ls[:, :256]] + [pltpu.roll(Ls, 768 - j, 1)[:, :256] for j in range(1, 7)]
    Rs = pltpu.roll(R, 642 + s, 1)[:, :640]
    Rj = [Rs[:, :512]] + [pltpu.roll(Rs, 640 - j, 1)[:, :512] for j in range(1, 7)]
    SL, _, IL = stats(Lj)
    _, MR, IR = stats(Rj)
    a = split3(-SL)
    b = split3(MR)
    pairs = ((0, 0), (0, 1), (1, 0), (1, 1), (0, 2), (2, 0))
    m = lax.broadcasted_iota(jnp.int32, (128, 128), 1) >= lax.broadcasted_iota(jnp.int32, (128, 128), 0)
    lane = lax.broadcasted_iota(jnp.int32, (1, 160), 1)
    place = jnp.where(lane < 112, lane % 16, (lane - 112) % 8)
    width = jnp.where(lane < 112, 6, 0)
    for blk in range(4):
        y0 = 8 * blk
        rt = jnp.concatenate([v[y0:y0 + 16].astype(BF16) for v in Rj]
                             + [jnp.concatenate([b[q][y0:y0 + 8].astype(F32) for _, q in pairs], 0).astype(BF16)], 0)
        lt = jnp.concatenate([v[y0:y0 + 16] for v in Lj]
                             + [a[p][y0:y0 + 8].astype(F32) for p, _ in pairs], 0)
        lc = lt.T.astype(BF16)
        for yy in range(8):
            y = y0 + yy
            keep = (place >= yy) & (place <= yy + width)
            lhs = lc * keep.astype(F32).astype(BF16)
            g = jnp.dot(lhs, rt, preferred_element_type=F32)
            for X in range(2):
                rows = slice(128 * X, 128 * X + 128)
                gi = [g[rows, 128 * (X + k):128 * (X + k + 1)] * IR[y:y + 1, 128 * (X + k):128 * (X + k + 1)]
                      for k in range(3)]
                one = jnp.where(m, gi[1], gi[2])
                more = jnp.where(m, gi[0], gi[1])
                v = jnp.where(two, jnp.maximum(one, more), one)
                acc_ref[rows, y:y + 1] = jnp.max(v, axis=1, keepdims=True)
    best = acc_ref[...].T[:32] * IL * (1.0 / 49.0)
    out_ref[...] = jnp.maximum(best, -2.0)


EXTRA = 384
SPAN = 768
MESH = pl.DeviceIdType.MESH


def exchange(l_ref, r_ref, out_ref, stage, own_sem, send_sem, recv_sem):
    band, tile = lax.axis_index("rows"), lax.axis_index("cols")
    bands, tiles = lax.axis_size("rows"), lax.axis_size("cols")
    above, below = lax.rem(band + bands - 1, bands), lax.rem(band + 1, bands)
    edge_up, edge_down = tile < 3, tile >= tiles - 3
    width = l_ref.shape[1]

    barrier = pltpu.get_barrier_semaphore()

    def greet(other_band, other_tile):
        pl.semaphore_signal(barrier, inc=1, device_id=(other_band, other_tile), device_id_type=MESH)

    @pl.loop(1, tiles)
    def _(k):
        greet(band, lax.rem(tile + k, tiles))

    for k in range(3):
        greet(above, tiles - 3 + k)
        greet(below, k)

    stage[:, :EXTRA] = jnp.zeros((2, EXTRA), stage.dtype)
    stage[:, EXTRA + width:] = jnp.zeros((2, EXTRA), stage.dtype)
    stage[0:1, EXTRA:EXTRA + width] = l_ref[...]
    stage[1:2, EXTRA:EXTRA + width] = r_ref[...]

    def window(other):
        return stage.at[:, pl.ds(pl.multiple_of(other * 256, 256), SPAN)]

    def send(other_band, other_tile, row, slot):
        pltpu.make_async_remote_copy(
            src_ref=window(other_tile), dst_ref=out_ref.at[row], send_sem=send_sem.at[slot], recv_sem=recv_sem,
            device_id=(other_band, other_tile), device_id_type=MESH).start()

    own = pltpu.make_async_copy(window(tile), out_ref.at[tile + 3], own_sem)
    own.start()

    on_edge = edge_up | edge_down
    pl.semaphore_wait(barrier, tiles - 1 + jnp.where(on_edge, tiles, 0))

    @pl.when(edge_up)
    def _():
        @pl.loop(0, tiles)
        def _(k):
            send(above, lax.rem(tile + k, tiles), tiles + 3 + tile, 1)

    @pl.when(edge_down)
    def _():
        @pl.loop(0, tiles)
        def _(k):
            send(below, lax.rem(tile + k, tiles), tile - (tiles - 3), 1)

    @pl.loop(1, tiles)
    def _(k):
        send(band, lax.rem(tile + k, tiles), tile + 3, 0)

    own.wait()

    def bytes_of(count, sem):
        return pltpu.make_async_copy(out_ref.at[pl.ds(0, count)], out_ref.at[pl.ds(0, count)], sem)

    bytes_of(tiles + 5, recv_sem).wait()
    bytes_of(tiles - 1, send_sem.at[0]).wait()

    @pl.when(on_edge)
    def _():
        bytes_of(tiles, send_sem.at[1]).wait()


def scores(rng_ref, w_ref, out_ref, acc_ref):
    band, tile = lax.axis_index("rows"), lax.axis_index("cols")
    line = lax.broadcasted_iota(jnp.int32, (40, SPAN), 0) + (32 * band - 3)
    inside = (line >= 0) & (line < 32 * lax.axis_size("rows")) & (line < 32 * band + 35)
    w = w_ref[...].astype(F32)
    left = jnp.where(inside, w[:, 0, :], 0.0)
    right = jnp.where(inside, w[:, 1, :], 0.0)
    compute(left, right, rng_ref[tile, 0], rng_ref[tile, 1] > 1, out_ref, acc_ref)


def solution(mesh):
    VMEM = pl.BlockSpec(memory_space=pltpu.VMEM)

    def on_device(left_image, right_image, ranges):
        windows = pl.pallas_call(
            exchange,
            out_shape=jax.ShapeDtypeStruct((40, 2, SPAN), BF16),
            in_specs=[VMEM, VMEM],
            out_specs=VMEM,
            scratch_shapes=[
                pltpu.VMEM((2, left_image.shape[1] + 2 * EXTRA), BF16),
                pltpu.SemaphoreType.DMA,
                pltpu.SemaphoreType.DMA((2,)),
                pltpu.SemaphoreType.DMA,
            ],
            name="exchange",
            compiler_params=pltpu.CompilerParams(collective_id=0, has_side_effects=True),
        )(left_image, right_image)
        return pl.pallas_call(
            scores,
            out_shape=jax.ShapeDtypeStruct((32, 256), F32),
            in_specs=[pl.BlockSpec(memory_space=pltpu.SMEM), VMEM],
            out_specs=VMEM,
            scratch_shapes=[pltpu.VMEM((256, 128), F32)],
            name="scores",
            compiler_params=pltpu.CompilerParams(vmem_limit_bytes=48 << 20),
        )(ranges, windows)

    return jax.shard_map(
        on_device,
        mesh=mesh,
        in_specs=(P(("rows", "cols"), None), P(("rows", "cols"), None), P()),
        out_specs=P("rows", "cols"),
        check_vma=False,
    )
```

```python
import jax
import jax.numpy as jnp
from jax import lax
from jax.experimental import pallas as pl
from jax.experimental.pallas import tpu as pltpu
from jax.sharding import PartitionSpec as P

F32, BF16 = jnp.float32, jnp.bfloat16

def split3(x):
    hi = x.astype(BF16)
    r = x - hi.astype(F32)
    mid = r.astype(BF16)
    lo = (r - mid.astype(F32)).astype(BF16)
    return hi, mid, lo

def box_rows(h):
    out = h[0:32]
    for i in range(1, 7):
        out = out + h[i:i + 32]
    return out

def stats(shifted):
    h = shifted[0]
    q = shifted[0] * shifted[0]
    for v in shifted[1:]:
        h = h + v
        q = q + v * v
    total = box_rows(h)
    mean = total * (1.0 / 49.0)
    spread = jnp.maximum(box_rows(q) * (1.0 / 49.0) - mean * mean, 0.01)
    return total, mean, lax.rsqrt(spread)

def compute(L, R, s, two, out_ref, acc_ref):
    Ls = pltpu.roll(L, 768 - 381, 1)
    Lj = [Ls[:, :256]] + [pltpu.roll(Ls, 768 - j, 1)[:, :256] for j in range(1, 7)]
    Rs = pltpu.roll(R, 642 + s, 1)[:, :640]
    Rj = [Rs[:, :512]] + [pltpu.roll(Rs, 640 - j, 1)[:, :512] for j in range(1, 7)]
    SL, _, IL = stats(Lj)
    _, MR, IR = stats(Rj)
    a = split3(-SL)
    b = split3(MR)
    pairs = ((0, 0), (0, 1), (1, 0), (1, 1), (0, 2), (2, 0))
    m = lax.broadcasted_iota(jnp.int32, (128, 128), 1) >= lax.broadcasted_iota(jnp.int32, (128, 128), 0)
    lane = lax.broadcasted_iota(jnp.int32, (1, 160), 1)
    place = jnp.where(lane < 112, lane % 16, (lane - 112) % 8)
    width = jnp.where(lane < 112, 6, 0)
    for blk in range(4):
        y0 = 8 * blk
        rt = jnp.concatenate([v[y0:y0 + 16].astype(BF16) for v in Rj]
                             + [jnp.concatenate([b[q][y0:y0 + 8].astype(F32) for _, q in pairs], 0).astype(BF16)], 0)
        lt = jnp.concatenate([v[y0:y0 + 16] for v in Lj]
                             + [a[p][y0:y0 + 8].astype(F32) for p, _ in pairs], 0)
        lc = lt.T.astype(BF16)
        for yy in range(8):
            y = y0 + yy
            keep = (place >= yy) & (place <= yy + width)
            lhs = lc * keep.astype(F32).astype(BF16)
            g = jnp.dot(lhs, rt, preferred_element_type=F32)
            for X in range(2):
                rows = slice(128 * X, 128 * X + 128)
                gi = [g[rows, 128 * (X + k):128 * (X + k + 1)] * IR[y:y + 1, 128 * (X + k):128 * (X + k + 1)]
                      for k in range(3)]
                one = jnp.where(m, gi[1], gi[2])
                more = jnp.where(m, gi[0], gi[1])
                v = jnp.where(two, jnp.maximum(one, more), one)
                acc_ref[rows, y:y + 1] = jnp.max(v, axis=1, keepdims=True)
    best = acc_ref[...].T[:32] * IL * (1.0 / 49.0)
    out_ref[...] = jnp.maximum(best, -2.0)


SPAN = 768
PAD = 384
MESH = pl.DeviceIdType.MESH
OFFSETS = sorted(((dy, dz) for dy in range(4) for dz in range(4)), key=lambda o: -(2 - abs(o[0] - 2)) - (2 - abs(o[1] - 2)))


def exchange(l_hbm, r_hbm, out_ref, l_row, r_row, stage, load_sem, own_sem, send_sem, recv_sem):
    band, tile = lax.axis_index("rows"), lax.axis_index("cols")
    bands, tiles = lax.axis_size("rows"), lax.axis_size("cols")
    width = l_hbm.shape[1]
    y, z, core = tile // 8, tile // 2 % 4, tile % 2
    goes_up = (tile < 3) & (band > 0)
    goes_down = (tile >= tiles - 3) & (band < bands - 1)
    other = jnp.where(goes_up, band - 1, band + 1)
    crosses = goes_up | goes_down
    barrier = pltpu.get_barrier_semaphore()

    loads = [pltpu.make_async_copy(l_hbm, l_row, load_sem.at[0]), pltpu.make_async_copy(r_hbm, r_row, load_sem.at[1])]
    for load in loads:
        load.start()

    def greet(other_band, other_tile):
        pl.semaphore_signal(barrier, inc=1, device_id=(other_band, other_tile), device_id_type=MESH)

    def peers(dy, dz):
        chip = (y + dy) % 4 * 8 + (z + dz) % 4 * 2
        return [chip + 1 - core] + ([chip + core] if dy or dz else [])

    @pl.when(band > 0)
    def _():
        for k in range(3):
            greet(band - 1, tiles - 3 + k)

    @pl.when(band < bands - 1)
    def _():
        for k in range(3):
            greet(band + 1, k)

    for dy, dz in OFFSETS:
        for peer in peers(dy, dz):
            greet(band, peer)

    for load in loads:
        load.wait()
    stage[:, :PAD] = jnp.zeros((2, PAD), stage.dtype)
    stage[:, PAD + width:] = jnp.zeros((2, PAD), stage.dtype)
    stage[0:1, PAD:PAD + width] = l_row[...]
    stage[1:2, PAD:PAD + width] = r_row[...]

    def window(peer):
        return stage.at[:, pl.ds(pl.multiple_of(peer * 256, 256), SPAN)]

    def send(other_band, peer, row, slot, kind):
        pltpu.make_async_remote_copy(
            src_ref=window(peer), dst_ref=out_ref.at[row], send_sem=send_sem.at[slot], recv_sem=recv_sem.at[kind],
            device_id=(other_band, peer), device_id_type=MESH).start()

    own = pltpu.make_async_copy(window(tile), out_ref.at[tile + 3], own_sem)
    own.start()
    pl.semaphore_wait(barrier, tiles - 1 + jnp.where(crosses, tiles, 0))
    row_there = jnp.where(goes_up, tiles + 3 + tile, tile - (tiles - 3))
    kind_there = jnp.where(goes_up, 2, 1)
    for dy, dz in OFFSETS:
        for peer in peers(dy, dz):
            send(band, peer, tile + 3, 0, 0)

        @pl.when(crosses)
        def _():
            chip = (y + dy) % 4 * 8 + (z + dz) % 4 * 2
            send(other, chip, row_there, 1, kind_there)
            send(other, chip + 1, row_there, 1, kind_there)

    def wait_for(count, sem):
        rows = out_ref.at[pl.ds(0, count)]
        pltpu.make_async_copy(rows, rows, sem).wait()

    own.wait()
    wait_for(tiles - 1, recv_sem.at[0])

    @pl.when(band > 0)
    def _():
        wait_for(3, recv_sem.at[1])

    @pl.when(band < bands - 1)
    def _():
        wait_for(3, recv_sem.at[2])

    wait_for(tiles - 1, send_sem.at[0])

    @pl.when(crosses)
    def _():
        wait_for(tiles, send_sem.at[1])


def scores(rng_ref, w_ref, out_ref, acc_ref):
    band, tile = lax.axis_index("rows"), lax.axis_index("cols")
    line = lax.broadcasted_iota(jnp.int32, (40, SPAN), 0) + (32 * band - 3)
    inside = (line >= 0) & (line < 32 * lax.axis_size("rows")) & (line < 32 * band + 35)
    w = w_ref[...].astype(F32)
    left = jnp.where(inside, w[:, 0, :], 0.0)
    right = jnp.where(inside, w[:, 1, :], 0.0)
    compute(left, right, rng_ref[0, tile], rng_ref[1, tile] > 1, out_ref, acc_ref)


def solution(mesh):
    VMEM = pl.BlockSpec(memory_space=pltpu.VMEM)

    def on_device(left_image, right_image, ranges):
        windows = pl.pallas_call(
            exchange,
            out_shape=jax.ShapeDtypeStruct((40, 2, SPAN), BF16),
            in_specs=[pl.BlockSpec(memory_space=pltpu.HBM)] * 2,
            out_specs=VMEM,
            scratch_shapes=[
                pltpu.VMEM(left_image.shape, BF16),
                pltpu.VMEM(right_image.shape, BF16),
                pltpu.VMEM((2, left_image.shape[1] + 2 * PAD), BF16),
                pltpu.SemaphoreType.DMA((2,)),
                pltpu.SemaphoreType.DMA,
                pltpu.SemaphoreType.DMA((2,)),
                pltpu.SemaphoreType.DMA((3,)),
            ],
            name="exchange",
            compiler_params=pltpu.CompilerParams(collective_id=0, has_side_effects=True, vmem_limit_bytes=4 << 20),
        )(*(pltpu.with_memory_space_constraint(x, pltpu.HBM) for x in (left_image, right_image)))
        return pl.pallas_call(
            scores,
            out_shape=jax.ShapeDtypeStruct((32, 256), F32),
            in_specs=[pl.BlockSpec(memory_space=pltpu.SMEM), VMEM],
            out_specs=VMEM,
            scratch_shapes=[pltpu.VMEM((256, 128), F32)],
            name="scores",
            compiler_params=pltpu.CompilerParams(vmem_limit_bytes=12 << 20),
        )(ranges.T, windows)

    return jax.shard_map(
        on_device,
        mesh=mesh,
        in_specs=(P(("rows", "cols"), None), P(("rows", "cols"), None), P()),
        out_specs=P("rows", "cols"),
        check_vma=False,
    )
```

```python
import jax
import jax.numpy as jnp
from jax import lax
from jax.experimental import pallas as pl
from jax.experimental.pallas import tpu as pltpu
from jax.sharding import PartitionSpec as P

F32, BF16 = jnp.float32, jnp.bfloat16

def split3(x):
    hi = x.astype(BF16)
    r = x - hi.astype(F32)
    mid = r.astype(BF16)
    lo = (r - mid.astype(F32)).astype(BF16)
    return hi, mid, lo

def box_rows(h):
    out = h[0:32]
    for i in range(1, 7):
        out = out + h[i:i + 32]
    return out

def stats(shifted):
    h = shifted[0]
    q = shifted[0] * shifted[0]
    for v in shifted[1:]:
        h = h + v
        q = q + v * v
    total = box_rows(h)
    mean = total * (1.0 / 49.0)
    spread = jnp.maximum(box_rows(q) * (1.0 / 49.0) - mean * mean, 0.01)
    return total, mean, lax.rsqrt(spread)

def compute(L, R, s, two, out_ref, acc_ref):
    Ls = pltpu.roll(L, 768 - 381, 1)
    Lj = [Ls[:, :256]] + [pltpu.roll(Ls, 768 - j, 1)[:, :256] for j in range(1, 7)]
    Rs = pltpu.roll(R, 642 + s, 1)[:, :640]
    Rj = [Rs[:, :512]] + [pltpu.roll(Rs, 640 - j, 1)[:, :512] for j in range(1, 7)]
    SL, _, IL = stats(Lj)
    _, MR, IR = stats(Rj)
    a = split3(-SL)
    b = split3(MR)
    pairs = ((0, 0), (0, 1), (1, 0), (1, 1), (0, 2), (2, 0))
    m = lax.broadcasted_iota(jnp.int32, (128, 128), 1) >= lax.broadcasted_iota(jnp.int32, (128, 128), 0)
    lane = lax.broadcasted_iota(jnp.int32, (1, 160), 1)
    place = jnp.where(lane < 112, lane % 16, (lane - 112) % 8)
    width = jnp.where(lane < 112, 6, 0)
    for blk in range(4):
        y0 = 8 * blk
        rt = jnp.concatenate([v[y0:y0 + 16].astype(BF16) for v in Rj]
                             + [jnp.concatenate([b[q][y0:y0 + 8].astype(F32) for _, q in pairs], 0).astype(BF16)], 0)
        lt = jnp.concatenate([v[y0:y0 + 16] for v in Lj]
                             + [a[p][y0:y0 + 8].astype(F32) for p, _ in pairs], 0)
        lc = lt.T.astype(BF16)
        for yy in range(8):
            y = y0 + yy
            keep = (place >= yy) & (place <= yy + width)
            lhs = lc * keep.astype(F32).astype(BF16)
            g = jnp.dot(lhs, rt, preferred_element_type=F32)
            for X in range(2):
                rows = slice(128 * X, 128 * X + 128)
                gi = [g[rows, 128 * (X + k):128 * (X + k + 1)] * IR[y:y + 1, 128 * (X + k):128 * (X + k + 1)]
                      for k in range(3)]
                one = jnp.where(m, gi[1], gi[2])
                more = jnp.where(m, gi[0], gi[1])
                v = jnp.where(two, jnp.maximum(one, more), one)
                acc_ref[rows, y:y + 1] = jnp.max(v, axis=1, keepdims=True)
    best = acc_ref[...].T[:32] * IL * (1.0 / 49.0)
    out_ref[...] = best


SPAN = 768
PAD = 384
MESH = pl.DeviceIdType.MESH
OFFSETS = sorted(((dy, dz) for dy in range(4) for dz in range(4)), key=lambda o: -(2 - abs(o[0] - 2)) - (2 - abs(o[1] - 2)))


def fused(rng_ref, l_hbm, r_hbm, best_ref, l_row, r_row, stage, out_ref, acc_ref, load_sem, own_sem, send_sem, recv_sem):
    band, tile = lax.axis_index("rows"), lax.axis_index("cols")
    bands, tiles = lax.axis_size("rows"), lax.axis_size("cols")
    width = l_hbm.shape[1]
    y, z, core = tile // 8, tile // 2 % 4, tile % 2
    goes_up = (tile < 3) & (band > 0)
    goes_down = (tile >= tiles - 3) & (band < bands - 1)
    other = jnp.where(goes_up, band - 1, band + 1)
    crosses = goes_up | goes_down
    barrier = pltpu.get_barrier_semaphore()

    loads = [pltpu.make_async_copy(l_hbm, l_row, load_sem.at[0]), pltpu.make_async_copy(r_hbm, r_row, load_sem.at[1])]
    for load in loads:
        load.start()

    def greet(other_band, other_tile):
        pl.semaphore_signal(barrier, inc=1, device_id=(other_band, other_tile), device_id_type=MESH)

    def peers(dy, dz):
        chip = (y + dy) % 4 * 8 + (z + dz) % 4 * 2
        return [chip + 1 - core] + ([chip + core] if dy or dz else [])

    @pl.when(band > 0)
    def _():
        for k in range(3):
            greet(band - 1, tiles - 3 + k)

    @pl.when(band < bands - 1)
    def _():
        for k in range(3):
            greet(band + 1, k)

    for dy, dz in OFFSETS:
        for peer in peers(dy, dz):
            greet(band, peer)

    for load in loads:
        load.wait()
    stage[:, :PAD] = jnp.zeros((2, PAD), stage.dtype)
    stage[:, PAD + width:] = jnp.zeros((2, PAD), stage.dtype)
    stage[0:1, PAD:PAD + width] = l_row[...]
    stage[1:2, PAD:PAD + width] = r_row[...]

    def window(peer):
        return stage.at[:, pl.ds(pl.multiple_of(peer * 256, 256), SPAN)]

    def send(other_band, peer, row, slot, kind):
        pltpu.make_async_remote_copy(
            src_ref=window(peer), dst_ref=out_ref.at[row], send_sem=send_sem.at[slot], recv_sem=recv_sem.at[kind],
            device_id=(other_band, peer), device_id_type=MESH).start()

    own = pltpu.make_async_copy(window(tile), out_ref.at[tile + 3], own_sem)
    own.start()
    pl.semaphore_wait(barrier, tiles - 1 + jnp.where(crosses, tiles, 0))
    row_there = jnp.where(goes_up, tiles + 3 + tile, tile - (tiles - 3))
    kind_there = jnp.where(goes_up, 2, 1)
    for dy, dz in OFFSETS:
        for peer in peers(dy, dz):
            send(band, peer, tile + 3, 0, 0)

        @pl.when(crosses)
        def _():
            chip = (y + dy) % 4 * 8 + (z + dz) % 4 * 2
            send(other, chip, row_there, 1, kind_there)
            send(other, chip + 1, row_there, 1, kind_there)

    def wait_for(count, sem):
        rows = out_ref.at[pl.ds(0, count)]
        pltpu.make_async_copy(rows, rows, sem).wait()

    own.wait()
    wait_for(tiles - 1, recv_sem.at[0])

    @pl.when(band > 0)
    def _():
        wait_for(3, recv_sem.at[1])

    @pl.when(band < bands - 1)
    def _():
        wait_for(3, recv_sem.at[2])

    line = lax.broadcasted_iota(jnp.int32, (40, SPAN), 0) + (32 * band - 3)
    inside = (line >= 0) & (line < 32 * bands) & (line < 32 * band + 35)
    w = out_ref[...].astype(F32)
    left = jnp.where(inside, w[:, 0, :], 0.0)
    right = jnp.where(inside, w[:, 1, :], 0.0)
    compute(left, right, rng_ref[0, tile], rng_ref[1, tile] > 1, best_ref, acc_ref)
    wait_for(tiles - 1, send_sem.at[0])

    @pl.when(crosses)
    def _():
        wait_for(tiles, send_sem.at[1])


def solution(mesh):
    VMEM = pl.BlockSpec(memory_space=pltpu.VMEM)

    def on_device(left_image, right_image, ranges):
        images = [pltpu.with_memory_space_constraint(x, pltpu.HBM) for x in (left_image, right_image)]
        best = pl.pallas_call(
            fused,
            out_shape=jax.ShapeDtypeStruct((32, 256), F32),
            in_specs=[pl.BlockSpec(memory_space=pltpu.SMEM)] + [pl.BlockSpec(memory_space=pltpu.HBM)] * 2,
            out_specs=VMEM,
            scratch_shapes=[
                pltpu.VMEM(left_image.shape, BF16),
                pltpu.VMEM(right_image.shape, BF16),
                pltpu.VMEM((2, left_image.shape[1] + 2 * PAD), BF16),
                pltpu.VMEM((40, 2, SPAN), BF16),
                pltpu.VMEM((256, 128), F32),
                pltpu.SemaphoreType.DMA((2,)),
                pltpu.SemaphoreType.DMA,
                pltpu.SemaphoreType.DMA((2,)),
                pltpu.SemaphoreType.DMA((3,)),
            ],
            name="exchange",
            compiler_params=pltpu.CompilerParams(collective_id=0, has_side_effects=True, vmem_limit_bytes=12 << 20),
        )(ranges.T, *images)
        return jnp.maximum(best, -2.0)

    return jax.shard_map(
        on_device,
        mesh=mesh,
        in_specs=(P(("rows", "cols"), None), P(("rows", "cols"), None), P()),
        out_specs=P("rows", "cols"),
        check_vma=False,
    )
```

```python
import jax
import jax.numpy as jnp
from jax import lax
from jax.experimental import pallas as pl
from jax.experimental.pallas import tpu as pltpu
from jax.sharding import PartitionSpec as P

F32, BF16 = jnp.float32, jnp.bfloat16
SPAN = 768
PAD = 384
MESH = pl.DeviceIdType.MESH
OFFSETS = sorted(((dy, dz) for dy in range(4) for dz in range(4)), key=lambda o: -(2 - abs(o[0] - 2)) - (2 - abs(o[1] - 2)))
PAIRS = ((0, 0), (0, 1), (1, 0), (1, 1), (0, 2), (2, 0))
TAPS = 7 * 24
DEPTH = TAPS + 8 * len(PAIRS)


def split3(x):
    hi = x.astype(BF16).astype(F32)
    mid = (x - hi).astype(BF16).astype(F32)
    return hi, mid, (x - hi) - mid


def joined(ref, tiles, *lead):
    return jnp.concatenate([ref[(*lead, pl.ds(pl.multiple_of(8 * t, 8), 8), slice(None))] for t in tiles], 0)


def kernel(rng_hbm, l_hbm, r_hbm, best_ref, rng, l_row, r_row, stage, win, lj, rj, lsum, rsum, acc, ordered,
           load_sem, own_sem, send_sem, recv_sem):
    band, tile = lax.axis_index("rows"), lax.axis_index("cols")
    bands, tiles = lax.axis_size("rows"), lax.axis_size("cols")
    width = l_hbm.shape[1]
    y, z, core = tile // 8, tile // 2 % 4, tile % 2
    goes_up = (tile < 3) & (band > 0)
    goes_down = (tile >= tiles - 3) & (band < bands - 1)
    other = jnp.where(goes_up, band - 1, band + 1)
    crosses = goes_up | goes_down
    barrier = pltpu.get_barrier_semaphore()

    loads = [pltpu.make_async_copy(a, b, load_sem.at[k])
             for k, (a, b) in enumerate(((l_hbm, l_row), (r_hbm, r_row), (rng_hbm, rng)))]
    for load in loads:
        load.start()

    def greet(other_band, other_tile):
        pl.semaphore_signal(barrier, inc=1, device_id=(other_band, other_tile), device_id_type=MESH)

    def peers(dy, dz):
        chip = (y + dy) % 4 * 8 + (z + dz) % 4 * 2
        return [chip + 1 - core] + ([chip + core] if dy or dz else [])

    @pl.when(band > 0)
    def _():
        for k in range(3):
            greet(band - 1, tiles - 3 + k)

    @pl.when(band < bands - 1)
    def _():
        for k in range(3):
            greet(band + 1, k)

    for dy, dz in OFFSETS:
        for peer in peers(dy, dz):
            greet(band, peer)

    for load in loads:
        load.wait()
    stage[:, :PAD] = jnp.zeros((2, PAD), stage.dtype)
    stage[:, PAD + width:] = jnp.zeros((2, PAD), stage.dtype)
    stage[0:1, PAD:PAD + width] = l_row[...]
    stage[1:2, PAD:PAD + width] = r_row[...]

    def window(peer):
        return stage.at[:, pl.ds(pl.multiple_of(peer * 256, 256), SPAN)]

    def send(other_band, peer, row, slot, kind):
        pltpu.make_async_remote_copy(
            src_ref=window(peer), dst_ref=win.at[row], send_sem=send_sem.at[slot], recv_sem=recv_sem.at[kind],
            device_id=(other_band, peer), device_id_type=MESH).start()

    own = pltpu.make_async_copy(window(tile), win.at[tile], own_sem)
    own.start()
    pl.semaphore_wait(barrier, tiles - 1 + jnp.where(crosses, tiles, 0))
    row_there = jnp.where(goes_up, tiles + tile, tile + 8)
    kind_there = jnp.where(goes_up, 5, 4)
    for dy, dz in OFFSETS:
        for peer in peers(dy, dz):
            send(band, peer, tile, 0, y)

        @pl.when(crosses)
        def _():
            chip = (y + dy) % 4 * 8 + (z + dz) % 4 * 2
            send(other, chip, row_there, 1, kind_there)
            send(other, chip + 1, row_there, 1, kind_there)

    def wait_for(count, sem):
        rows = win.at[pl.ds(0, count)]
        pltpu.make_async_copy(rows, rows, sem).wait()

    start = rng[0, tile]
    two = rng[1, tile] > 1

    def prepare(group, inside=None):
        w = win[pl.ds(8 * group, 8)].astype(F32)
        left, right = w[:, 0, :], w[:, 1, :]
        if inside is not None:
            left, right = jnp.where(inside, left, 0.0), jnp.where(inside, right, 0.0)
        rows = pl.ds(pl.multiple_of(8 * group, 8), 8)
        left = pltpu.roll(left, SPAN - 381, 1)
        right = pltpu.roll(right, 642 + start, 1)[:, :640]
        for ref, sums, x, cols in ((lj, lsum, left, 256), (rj, rsum, right, 512)):
            total = square = 0.0
            for j in range(7):
                v = (pltpu.roll(x, x.shape[1] - j, 1) if j else x)[:, :cols]
                ref[j, rows, :] = v
                total, square = total + v, square + v * v
            sums[0, rows, :] = total
            sums[1, rows, :] = square

    sub = lax.broadcasted_iota(jnp.int32, (8, SPAN), 0)
    halo_rows = ((sub < 3) & (band < bands - 1)) | ((sub >= 5) & (band > 0))

    def prepare_halo():
        @pl.when(band > 0)
        def _():
            wait_for(3, recv_sem.at[4])

        @pl.when(band < bands - 1)
        def _():
            wait_for(3, recv_sem.at[5])

        prepare(4, halo_rows)

    upper = lax.broadcasted_iota(jnp.int32, (128, 128), 1) >= lax.broadcasted_iota(jnp.int32, (128, 128), 0)
    lane = lax.broadcasted_iota(jnp.int32, (1, DEPTH), 1)
    place = jnp.where(lane < TAPS, lane % 24, 100 + (lane - TAPS) % 8)

    def block(step, g):
        wraps = g == 3
        trio = (g, g + 1, jnp.where(wraps, 0, g))

        def box(sums, i, cols):
            h = joined(sums, trio, i)
            near, far = h[0:8], h[8:16]
            for k in range(1, 7):
                near, far = near + h[k:k + 8], far + h[8 + k:16 + k]
            return jnp.where((sub[:, :cols] >= 5) & wraps, far, near)

        def stats(sums, cols):
            total = box(sums, 0, cols)
            mean = total * (1.0 / 49.0)
            spread = jnp.maximum(box(sums, 1, cols) * (1.0 / 49.0) - mean * mean, 0.01)
            return total, mean, lax.rsqrt(spread)

        total_l, _, scale_l = stats(lsum, 256)
        _, mean_r, scale_r = stats(rsum, 512)
        a, b = split3(-total_l), split3(mean_r)
        rt = jnp.concatenate([joined(rj, trio, j) for j in range(7)] + [b[q] for _, q in PAIRS], 0).astype(BF16)
        lt = jnp.concatenate([joined(lj, trio, j) for j in range(7)] + [a[p] for p, _ in PAIRS], 0).T.astype(BF16)
        for k in range(8):
            first = k + (jnp.where(wraps, 8, 0) if k >= 5 else 0)
            keep = ((place >= first) & (place <= first + 6)) | (place == 100 + k)
            g7 = jnp.dot(lt * keep.astype(F32).astype(BF16), rt, preferred_element_type=F32)
            for half in range(2):
                rows = slice(128 * half, 128 * half + 128)
                part = [slice(128 * (half + i), 128 * (half + i + 1)) for i in range(3)]
                s = [g7[rows, c] * scale_r[k:k + 1, c] for c in part]
                one, more = jnp.where(upper, s[1], s[2]), jnp.where(upper, s[0], s[1])
                v = jnp.where(two, jnp.maximum(one, more), one)
                acc[rows, 8 * step + k:8 * step + k + 1] = jnp.max(v, axis=1, keepdims=True)
        return scale_l * (1.0 / 49.0)

    blocks = [(y + 3 + step) % 4 for step in range(4)]
    scales = []
    own.wait()
    wait_for(7, recv_sem.at[y])
    wait_for(8, recv_sem.at[blocks[0]])
    prepare(y)
    prepare(blocks[0])
    pl.when(blocks[0] == 3)(prepare_halo)
    scales.append(block(0, blocks[0]))
    wait_for(8, recv_sem.at[blocks[2]])
    prepare(blocks[2])
    pl.when(blocks[1] == 3)(prepare_halo)
    scales.append(block(1, blocks[1]))
    wait_for(8, recv_sem.at[blocks[3]])
    prepare(blocks[3])
    pl.when((blocks[2] == 3) | (blocks[3] == 3))(prepare_halo)
    scales.append(block(2, blocks[2]))
    scales.append(block(3, blocks[3]))
    best = acc[...].T[:32]
    for step in range(4):
        ordered[pl.ds(pl.multiple_of(8 * blocks[step], 8), 8), :] = best[8 * step:8 * step + 8] * scales[step]
    best_ref[...] = pltpu.roll(ordered[...], 3, 0)

    wait_for(tiles - 1, send_sem.at[0])

    @pl.when(crosses)
    def _():
        wait_for(tiles, send_sem.at[1])


def solution(mesh):
    def on_device(left_image, right_image, ranges):
        arrays = [pltpu.with_memory_space_constraint(x, pltpu.HBM) for x in (ranges.T, left_image, right_image)]
        best = pl.pallas_call(
            kernel,
            out_shape=jax.ShapeDtypeStruct((32, 256), F32),
            in_specs=[pl.BlockSpec(memory_space=pltpu.HBM)] * 3,
            out_specs=pl.BlockSpec(memory_space=pltpu.VMEM),
            scratch_shapes=[
                pltpu.SMEM((2, 32), jnp.int32),
                pltpu.VMEM(left_image.shape, BF16),
                pltpu.VMEM(right_image.shape, BF16),
                pltpu.VMEM((2, left_image.shape[1] + 2 * PAD), BF16),
                pltpu.VMEM((40, 2, SPAN), BF16),
                pltpu.VMEM((7, 40, 256), F32),
                pltpu.VMEM((7, 40, 512), F32),
                pltpu.VMEM((2, 40, 256), F32),
                pltpu.VMEM((2, 40, 512), F32),
                pltpu.VMEM((256, 128), F32),
                pltpu.VMEM((32, 256), F32),
                pltpu.SemaphoreType.DMA((3,)),
                pltpu.SemaphoreType.DMA,
                pltpu.SemaphoreType.DMA((2,)),
                pltpu.SemaphoreType.DMA((6,)),
            ],
            name="match",
            compiler_params=pltpu.CompilerParams(collective_id=0, has_side_effects=True, vmem_limit_bytes=16 << 20),
        )(*arrays)
        return jnp.maximum(best, -2.0)

    return jax.shard_map(
        on_device,
        mesh=mesh,
        in_specs=(P(("rows", "cols"), None), P(("rows", "cols"), None), P()),
        out_specs=P("rows", "cols"),
        check_vma=False,
    )
```

```python
import jax
import jax.numpy as jnp
from jax import lax
from jax.experimental import pallas as pl
from jax.experimental.pallas import tpu as pltpu
from jax.sharding import PartitionSpec as P

F32, BF16 = jnp.float32, jnp.bfloat16
SPAN = 768
PAD = 384
MESH = pl.DeviceIdType.MESH
OFFSETS = sorted(((dy, dz) for dy in range(4) for dz in range(4)), key=lambda o: -(2 - abs(o[0] - 2)) - (2 - abs(o[1] - 2)))
PAIRS = ((0, 0), (0, 1), (1, 0), (1, 1), (0, 2), (2, 0))


def split3(x):
    hi = x.astype(BF16).astype(F32)
    mid = (x - hi).astype(BF16).astype(F32)
    return hi, mid, (x - hi) - mid


def joined(ref, tiles, *lead):
    return jnp.concatenate([ref[(*lead, slice(8 * t, 8 * t + 8), slice(None))] for t in tiles], 0)


def kernel(rng_hbm, l_hbm, r_hbm, best_ref, rng, l_row, r_row, stage, win, lj, rj, lsum, rsum, acc,
           load_sem, send_sem, recv_sem):
    band, tile = lax.axis_index("rows"), lax.axis_index("cols")
    bands, tiles = lax.axis_size("rows"), lax.axis_size("cols")
    width = l_hbm.shape[1]
    y, z, core = tile // 8, tile // 2 % 4, tile % 2
    goes_up = (tile < 3) & (band > 0)
    goes_down = (tile >= tiles - 3) & (band < bands - 1)
    other = jnp.where(goes_up, band - 1, band + 1)
    crosses = goes_up | goes_down
    barrier = pltpu.get_barrier_semaphore()

    loads = [pltpu.make_async_copy(a, b, load_sem.at[k])
             for k, (a, b) in enumerate(((l_hbm, l_row), (r_hbm, r_row), (rng_hbm, rng)))]
    for load in loads:
        load.start()

    def greet(other_band, other_tile):
        pl.semaphore_signal(barrier, inc=1, device_id=(other_band, other_tile), device_id_type=MESH)

    def peers(dy, dz):
        chip = (y + dy) % 4 * 8 + (z + dz) % 4 * 2
        return [chip + 1 - core] + ([chip + core] if dy or dz else [])

    @pl.when(band > 0)
    def _():
        for k in range(3):
            greet(band - 1, tiles - 3 + k)

    @pl.when(band < bands - 1)
    def _():
        for k in range(3):
            greet(band + 1, k)

    for dy, dz in OFFSETS:
        for peer in peers(dy, dz):
            greet(band, peer)

    for load in loads:
        load.wait()
    stage[:, :PAD] = jnp.zeros((2, PAD), stage.dtype)
    stage[:, PAD + width:] = jnp.zeros((2, PAD), stage.dtype)
    stage[0:1, PAD:PAD + width] = l_row[...]
    stage[1:2, PAD:PAD + width] = r_row[...]

    def window(peer):
        return stage.at[:, pl.ds(pl.multiple_of(peer * 256, 256), SPAN)]

    def send(other_band, peer, row, slot, kind):
        pltpu.make_async_remote_copy(
            src_ref=window(peer), dst_ref=win.at[row], send_sem=send_sem.at[slot], recv_sem=recv_sem.at[kind],
            device_id=(other_band, peer), device_id_type=MESH).start()

    pltpu.make_async_copy(window(tile), win.at[tile], recv_sem.at[y]).start()
    pl.semaphore_wait(barrier, tiles - 1 + jnp.where(crosses, tiles, 0))
    row_there = jnp.where(goes_up, tiles + tile, tile + 8)
    kind_there = jnp.where(goes_up, 5, 4)
    for dy, dz in OFFSETS:
        for peer in peers(dy, dz):
            send(band, peer, tile, 0, y)

        @pl.when(crosses)
        def _():
            chip = (y + dy) % 4 * 8 + (z + dz) % 4 * 2
            send(other, chip, row_there, 1, kind_there)
            send(other, chip + 1, row_there, 1, kind_there)

    def wait_for(count, sem):
        rows = win.at[pl.ds(0, count)]
        pltpu.make_async_copy(rows, rows, sem).wait()

    start = rng[0, tile]
    two = rng[1, tile] > 1

    def prepare(group, inside=None):
        w = win[8 * group:8 * group + 8].astype(F32)
        left, right = w[:, 0, :], w[:, 1, :]
        if inside is not None:
            left, right = jnp.where(inside, left, 0.0), jnp.where(inside, right, 0.0)
        rows = slice(8 * group, 8 * group + 8)
        left = pltpu.roll(left, SPAN - 381, 1)
        right = pltpu.roll(right, 642 + start, 1)[:, :640]
        for ref, sums, x, cols in ((lj, lsum, left, 256), (rj, rsum, right, 512)):
            total = square = 0.0
            for j in range(7):
                v = (pltpu.roll(x, x.shape[1] - j, 1) if j else x)[:, :cols]
                ref[j, rows, :] = v
                total, square = total + v, square + v * v
            sums[0, rows, :] = total
            sums[1, rows, :] = square

    sub = lax.broadcasted_iota(jnp.int32, (8, SPAN), 0)
    halo_rows = ((sub < 3) & (band < bands - 1)) | ((sub >= 5) & (band > 0))

    def prepare_halo():
        @pl.when(band > 0)
        def _():
            wait_for(3, recv_sem.at[4])

        @pl.when(band < bands - 1)
        def _():
            wait_for(3, recv_sem.at[5])

        prepare(4, halo_rows)

    upper = lax.broadcasted_iota(jnp.int32, (128, 128), 1) >= lax.broadcasted_iota(jnp.int32, (128, 128), 0)

    def operands(trio):
        wraps = len(trio) == 3

        def box(sums, i, cols):
            h = joined(sums, trio, i)
            near = h[0:8]
            for k in range(1, 7):
                near = near + h[k:k + 8]
            if not wraps:
                return near
            far = h[8:16]
            for k in range(1, 7):
                far = far + h[8 + k:16 + k]
            return jnp.where(sub[:, :cols] >= 5, far, near)

        def stats(sums, cols):
            total = box(sums, 0, cols)
            mean = total * (1.0 / 49.0)
            spread = jnp.maximum(box(sums, 1, cols) * (1.0 / 49.0) - mean * mean, 0.01)
            return total, mean, lax.rsqrt(spread)

        total_l, _, scale_l = stats(lsum, 256)
        _, mean_r, scale_r = stats(rsum, 512)
        a, b = split3(-total_l), split3(mean_r)
        rt = jnp.concatenate([joined(rj, trio, j) for j in range(7)] + [b[q] for _, q in PAIRS], 0).astype(BF16)
        lt = jnp.concatenate([joined(lj, trio, j) for j in range(7)] + [a[p] for p, _ in PAIRS], 0).T.astype(BF16)
        return 8 * len(trio), lt, rt, scale_l * (1.0 / 49.0), scale_r

    def block(step, taps, lt, rt, scale_l, scale_r):
        lane = lax.broadcasted_iota(jnp.int32, (1, lt.shape[1]), 1)
        place = jnp.where(lane < 7 * taps, lane % taps, 100 + (lane - 7 * taps) % 8)
        for k in range(8):
            first = k + (8 if taps == 24 and k >= 5 else 0)
            keep = ((place >= first) & (place <= first + 6)) | (place == 100 + k)
            g = jnp.dot(lt * keep.astype(F32).astype(BF16), rt, preferred_element_type=F32)
            for half in range(2):
                rows = slice(128 * half, 128 * half + 128)
                part = [slice(128 * (half + i), 128 * (half + i + 1)) for i in range(3)]
                s = [g[rows, c] * scale_r[k:k + 1, c] for c in part]
                one, more = jnp.where(upper, s[1], s[2]), jnp.where(upper, s[0], s[1])
                v = jnp.where(two, jnp.maximum(one, more), one)
                acc[rows, 8 * step + k:8 * step + k + 1] = jnp.max(v, axis=1, keepdims=True)

    for group in range(4):
        wait_for(8, recv_sem.at[group])
        prepare(group)
    parts = [operands((0, 1)), operands((1, 2)), operands((2, 3))]
    block(0, *parts[0])
    block(1, *parts[1])
    prepare_halo()
    parts.append(operands((3, 4, 0)))
    block(2, *parts[2])
    block(3, *parts[3])
    best = acc[...].T[:32] * jnp.concatenate([p[3] for p in parts], 0)
    best_ref[...] = pltpu.roll(best, 3, 0)

    wait_for(tiles - 1, send_sem.at[0])

    @pl.when(crosses)
    def _():
        wait_for(tiles, send_sem.at[1])


def solution(mesh):
    def on_device(left_image, right_image, ranges):
        arrays = [pltpu.with_memory_space_constraint(x, pltpu.HBM) for x in (ranges.T, left_image, right_image)]
        best = pl.pallas_call(
            kernel,
            out_shape=jax.ShapeDtypeStruct((32, 256), F32),
            in_specs=[pl.BlockSpec(memory_space=pltpu.HBM)] * 3,
            out_specs=pl.BlockSpec(memory_space=pltpu.VMEM),
            scratch_shapes=[
                pltpu.SMEM((2, 32), jnp.int32),
                pltpu.VMEM(left_image.shape, BF16),
                pltpu.VMEM(right_image.shape, BF16),
                pltpu.VMEM((2, left_image.shape[1] + 2 * PAD), BF16),
                pltpu.VMEM((40, 2, SPAN), BF16),
                pltpu.VMEM((7, 40, 256), F32),
                pltpu.VMEM((7, 40, 512), F32),
                pltpu.VMEM((2, 40, 256), F32),
                pltpu.VMEM((2, 40, 512), F32),
                pltpu.VMEM((256, 128), F32),
                pltpu.SemaphoreType.DMA((3,)),
                pltpu.SemaphoreType.DMA((2,)),
                pltpu.SemaphoreType.DMA((6,)),
            ],
            name="match",
            compiler_params=pltpu.CompilerParams(collective_id=0, has_side_effects=True, vmem_limit_bytes=16 << 20),
        )(*arrays)
        return jnp.maximum(best, -2.0)

    return jax.shard_map(
        on_device,
        mesh=mesh,
        in_specs=(P(("rows", "cols"), None), P(("rows", "cols"), None), P()),
        out_specs=P("rows", "cols"),
        check_vma=False,
    )
```

```python
import jax
import jax.numpy as jnp
from jax import lax
from jax.experimental import pallas as pl
from jax.experimental.pallas import tpu as pltpu
from jax.sharding import PartitionSpec as P

F32, BF16 = jnp.float32, jnp.bfloat16
SPAN = 768
PAD = 384
MESH = pl.DeviceIdType.MESH
OFFSETS = sorted(((dy, dz) for dy in range(4) for dz in range(4)), key=lambda o: -(2 - abs(o[0] - 2)) - (2 - abs(o[1] - 2)))
PAIRS = ((0, 0), (0, 1), (1, 0), (1, 1), (0, 2), (2, 0))


def split3(x):
    hi = x.astype(BF16).astype(F32)
    mid = (x - hi).astype(BF16).astype(F32)
    return hi, mid, (x - hi) - mid


def joined(ref, tiles, *lead):
    return jnp.concatenate([ref[(*lead, slice(8 * t, 8 * t + 8), slice(None))] for t in tiles], 0)


def kernel(rng_hbm, l_hbm, r_hbm, best_ref, rng, l_row, r_row, stage, win, lj, rj, lsum, rsum, acc,
           load_sem, send_sem, recv_sem, go):
    band, tile = lax.axis_index("rows"), lax.axis_index("cols")
    bands, tiles = lax.axis_size("rows"), lax.axis_size("cols")
    width = l_hbm.shape[1]
    y, z, core = tile // 8, tile // 2 % 4, tile % 2
    goes_up = (tile < 3) & (band > 0)
    goes_down = (tile >= tiles - 3) & (band < bands - 1)
    other = jnp.where(goes_up, band - 1, band + 1)
    crosses = goes_up | goes_down
    asked = ((tile < 3) & (band < bands - 1)) | ((tile >= tiles - 3) & (band > 0))
    asker = jnp.where(tile < 3, band + 1, band - 1)
    barrier = pltpu.get_barrier_semaphore()

    loads = [pltpu.make_async_copy(a, b, load_sem.at[k])
             for k, (a, b) in enumerate(((l_hbm, l_row), (r_hbm, r_row), (rng_hbm, rng)))]

    def greet(other_band, other_tile):
        pl.semaphore_signal(barrier, inc=1, device_id=(other_band, other_tile), device_id_type=MESH)

    def peers(dy, dz):
        chip = (y + dy) % 4 * 8 + (z + dz) % 4 * 2
        return [chip + 1 - core] + ([chip + core] if dy or dz else [])

    @pl.when(crosses)
    def _():
        greet(other, tile)

    for dy, dz in OFFSETS:
        for peer in peers(dy, dz):
            greet(band, peer)

    for load in loads:
        load.start()
    for load in loads:
        load.wait()
    stage[:, :PAD] = jnp.zeros((2, PAD), stage.dtype)
    stage[:, PAD + width:] = jnp.zeros((2, PAD), stage.dtype)
    stage[0:1, PAD:PAD + width] = l_row[...]
    stage[1:2, PAD:PAD + width] = r_row[...]

    def window(peer):
        return stage.at[:, pl.ds(pl.multiple_of(peer * 256, 256), SPAN)]

    def send(other_band, peer, row, slot, kind):
        pltpu.make_async_remote_copy(
            src_ref=window(peer), dst_ref=win.at[row], send_sem=send_sem.at[slot], recv_sem=recv_sem.at[kind],
            device_id=(other_band, peer), device_id_type=MESH).start()

    pltpu.make_async_copy(window(tile), win.at[tile], recv_sem.at[y]).start()
    pl.semaphore_wait(barrier, tiles - 1 + asked.astype(jnp.int32))

    @pl.when(asked)
    def _():
        pl.semaphore_signal(go, inc=1, device_id=(asker, tile), device_id_type=MESH)

    row_there = jnp.where(goes_up, tiles + tile, tile + 8)
    kind_there = jnp.where(goes_up, 5, 4)
    for dy, dz in OFFSETS:
        for peer in peers(dy, dz):
            send(band, peer, tile, 0, y)

    @pl.when(crosses)
    def _():
        pl.semaphore_wait(go, 1)
        for dy, dz in OFFSETS:
            chip = (y + dy) % 4 * 8 + (z + dz) % 4 * 2
            send(other, chip, row_there, 1, kind_there)
            send(other, chip + 1, row_there, 1, kind_there)

    def wait_for(count, sem):
        rows = win.at[pl.ds(0, count)]
        pltpu.make_async_copy(rows, rows, sem).wait()

    start = rng[0, tile]
    two = rng[1, tile] > 1

    within = lax.broadcasted_iota(jnp.int32, (8, 128), 1) < 2 + start

    def prepare(group, inside=None):
        w = win[8 * group:8 * group + 8].astype(F32)
        left, right = w[:, 0, :], w[:, 1, :]
        if inside is not None:
            left, right = jnp.where(inside, left, 0.0), jnp.where(inside, right, 0.0)
        rows = slice(8 * group, 8 * group + 8)
        left = pltpu.roll(left, SPAN - 381, 1)
        spun = [pltpu.roll(right[:, 128 * i:128 * i + 128], 2 + start, 1) for i in range(6)]
        right = jnp.concatenate([jnp.where(within, a, b) for a, b in zip(spun, spun[1:])], 1)
        for ref, sums, x, cols in ((lj, lsum, left, 256), (rj, rsum, right, 512)):
            total = square = 0.0
            for j in range(7):
                v = (pltpu.roll(x, x.shape[1] - j, 1) if j else x)[:, :cols]
                ref[j, rows, :] = v
                total, square = total + v, square + v * v
            sums[0, rows, :] = total
            sums[1, rows, :] = square

    sub = lax.broadcasted_iota(jnp.int32, (8, SPAN), 0)
    halo_rows = ((sub < 3) & (band < bands - 1)) | ((sub >= 5) & (band > 0))

    def wait_halo():
        @pl.when(band > 0)
        def _():
            wait_for(3, recv_sem.at[4])

        @pl.when(band < bands - 1)
        def _():
            wait_for(3, recv_sem.at[5])


    upper = lax.broadcasted_iota(jnp.int32, (128, 128), 1) >= lax.broadcasted_iota(jnp.int32, (128, 128), 0)

    def operands(trio):
        wraps = len(trio) == 3

        def box(sums, i, cols):
            h = joined(sums, trio, i)
            near = h[0:8]
            for k in range(1, 7):
                near = near + h[k:k + 8]
            if not wraps:
                return near
            far = h[8:16]
            for k in range(1, 7):
                far = far + h[8 + k:16 + k]
            return jnp.where(sub[:, :cols] >= 5, far, near)

        def stats(sums, cols):
            total = box(sums, 0, cols)
            mean = total * (1.0 / 49.0)
            spread = jnp.maximum(box(sums, 1, cols) * (1.0 / 49.0) - mean * mean, 0.01)
            return total, mean, lax.rsqrt(spread)

        total_l, _, scale_l = stats(lsum, 256)
        _, mean_r, scale_r = stats(rsum, 512)
        a, b = split3(-total_l), split3(mean_r)
        rt = jnp.concatenate([joined(rj, trio, j) for j in range(7)] + [b[q] for _, q in PAIRS], 0).astype(BF16)
        lt = jnp.concatenate([joined(lj, trio, j) for j in range(7)] + [a[p] for p, _ in PAIRS], 0).T.astype(BF16)
        return 8 * len(trio), lt, rt, scale_l * (1.0 / 49.0), scale_r

    def block(step, taps, lt, rt, scale_l, scale_r):
        lane = lax.broadcasted_iota(jnp.int32, (1, lt.shape[1]), 1)
        place = jnp.where(lane < 7 * taps, lane % taps, 100 + (lane - 7 * taps) % 8)
        for k in range(8):
            first = k + (8 if taps == 24 and k >= 5 else 0)
            keep = ((place >= first) & (place <= first + 6)) | (place == 100 + k)
            g = jnp.dot(lt * keep.astype(F32).astype(BF16), rt, preferred_element_type=F32)
            for half in range(2):
                rows = slice(128 * half, 128 * half + 128)
                part = [slice(128 * (half + i), 128 * (half + i + 1)) for i in range(3)]
                s = [g[rows, c] * scale_r[k:k + 1, c] for c in part]
                one, more = jnp.where(upper, s[1], s[2]), jnp.where(upper, s[0], s[1])
                v = jnp.where(two, jnp.maximum(one, more), one)
                acc[rows, 8 * step + k:8 * step + k + 1] = jnp.max(v, axis=1, keepdims=True)

    wait_for(8, recv_sem.at[0])
    prepare(0)
    wait_for(8, recv_sem.at[1])
    prepare(1)
    wait_for(8, recv_sem.at[2])
    prepare(2)
    wait_for(8, recv_sem.at[3])
    prepare(3)
    parts = [operands((0, 1))]
    parts.append(operands((1, 2)))
    parts.append(operands((2, 3)))
    block(0, *parts[0])
    wait_halo()
    prepare(4, halo_rows)
    parts.append(operands((3, 4, 0)))
    block(1, *parts[1])
    block(2, *parts[2])
    block(3, *parts[3])
    best = acc[...].T[:32] * jnp.concatenate([p[3] for p in parts], 0)
    best_ref[...] = pltpu.roll(best, 3, 0)

    wait_for(tiles - 1, send_sem.at[0])

    @pl.when(crosses)
    def _():
        wait_for(tiles, send_sem.at[1])


def solution(mesh):
    def on_device(left_image, right_image, ranges):
        arrays = [pltpu.with_memory_space_constraint(x, pltpu.HBM) for x in (ranges.T, left_image, right_image)]
        best = pl.pallas_call(
            kernel,
            out_shape=jax.ShapeDtypeStruct((32, 256), F32),
            in_specs=[pl.BlockSpec(memory_space=pltpu.HBM)] * 3,
            out_specs=pl.BlockSpec(memory_space=pltpu.VMEM),
            scratch_shapes=[
                pltpu.SMEM((2, 32), jnp.int32),
                pltpu.VMEM(left_image.shape, BF16),
                pltpu.VMEM(right_image.shape, BF16),
                pltpu.VMEM((2, left_image.shape[1] + 2 * PAD), BF16),
                pltpu.VMEM((40, 2, SPAN), BF16),
                pltpu.VMEM((7, 40, 256), F32),
                pltpu.VMEM((7, 40, 512), F32),
                pltpu.VMEM((2, 40, 256), F32),
                pltpu.VMEM((2, 40, 512), F32),
                pltpu.VMEM((256, 128), F32),
                pltpu.SemaphoreType.DMA((3,)),
                pltpu.SemaphoreType.DMA((2,)),
                pltpu.SemaphoreType.DMA((6,)),
                pltpu.SemaphoreType.REGULAR,
            ],
            name="match",
            compiler_params=pltpu.CompilerParams(collective_id=0, has_side_effects=True, vmem_limit_bytes=16 << 20),
        )(*arrays)
        return jnp.maximum(best, -2.0)

    return jax.shard_map(
        on_device,
        mesh=mesh,
        in_specs=(P(("rows", "cols"), None), P(("rows", "cols"), None), P()),
        out_specs=P("rows", "cols"),
        check_vma=False,
    )
```

```python
import jax
import jax.numpy as jnp
from jax import lax
from jax.experimental import pallas as pl
from jax.experimental.pallas import tpu as pltpu
from jax.sharding import PartitionSpec as P

F32, BF16 = jnp.float32, jnp.bfloat16
SPAN = 768
PAD = 384
MESH = pl.DeviceIdType.MESH
OFFSETS = sorted(((dy, dz) for dy in range(4) for dz in range(4)), key=lambda o: -(2 - abs(o[0] - 2)) - (2 - abs(o[1] - 2)))
PAIRS = ((0, 0), (0, 1), (1, 0), (1, 1), (0, 2), (2, 0))


def split3(x):
    hi = x.astype(BF16).astype(F32)
    mid = (x - hi).astype(BF16).astype(F32)
    return hi, mid, (x - hi) - mid


def joined(ref, tiles, *lead):
    return jnp.concatenate([ref[(*lead, slice(8 * t, 8 * t + 8), slice(None))] for t in tiles], 0)


def kernel(rng_hbm, l_hbm, r_hbm, best_ref, rng, l_row, r_row, stage, win, lj, rj, lsum, rsum, tops,
           load_sem, send_sem, recv_sem, go):
    band, tile = lax.axis_index("rows"), lax.axis_index("cols")
    bands, tiles = lax.axis_size("rows"), lax.axis_size("cols")
    width = l_hbm.shape[1]
    y, z, core = tile // 8, tile // 2 % 4, tile % 2
    goes_up = (tile < 3) & (band > 0)
    goes_down = (tile >= tiles - 3) & (band < bands - 1)
    other = jnp.where(goes_up, band - 1, band + 1)
    crosses = goes_up | goes_down
    asked = ((tile < 3) & (band < bands - 1)) | ((tile >= tiles - 3) & (band > 0))
    asker = jnp.where(tile < 3, band + 1, band - 1)
    barrier = pltpu.get_barrier_semaphore()

    loads = [pltpu.make_async_copy(a, b, load_sem.at[k])
             for k, (a, b) in enumerate(((l_hbm, l_row), (r_hbm, r_row), (rng_hbm, rng)))]

    def greet(other_band, other_tile):
        pl.semaphore_signal(barrier, inc=1, device_id=(other_band, other_tile), device_id_type=MESH)

    def peers(dy, dz):
        chip = (y + dy) % 4 * 8 + (z + dz) % 4 * 2
        return [chip + 1 - core] + ([chip + core] if dy or dz else [])

    @pl.when(crosses)
    def _():
        greet(other, tile)

    for dy, dz in OFFSETS:
        for peer in peers(dy, dz):
            greet(band, peer)

    for load in loads:
        load.start()
    for load in loads:
        load.wait()
    stage[:, :PAD] = jnp.zeros((2, PAD), stage.dtype)
    stage[:, PAD + width:] = jnp.zeros((2, PAD), stage.dtype)
    stage[0:1, PAD:PAD + width] = l_row[...]
    stage[1:2, PAD:PAD + width] = r_row[...]

    def window(peer):
        return stage.at[:, pl.ds(pl.multiple_of(peer * 256, 256), SPAN)]

    def send(other_band, peer, row, slot, kind):
        pltpu.make_async_remote_copy(
            src_ref=window(peer), dst_ref=win.at[row], send_sem=send_sem.at[slot], recv_sem=recv_sem.at[kind],
            device_id=(other_band, peer), device_id_type=MESH).start()

    pltpu.make_async_copy(window(tile), win.at[tile], recv_sem.at[y]).start()
    pl.semaphore_wait(barrier, tiles - 1 + asked.astype(jnp.int32))

    @pl.when(asked)
    def _():
        pl.semaphore_signal(go, inc=1, device_id=(asker, tile), device_id_type=MESH)

    row_there = jnp.where(goes_up, tiles + tile, tile + 8)
    kind_there = jnp.where(goes_up, 5, 4)
    for dy, dz in OFFSETS:
        for peer in peers(dy, dz):
            send(band, peer, tile, 0, y)

    @pl.when(crosses)
    def _():
        pl.semaphore_wait(go, 1)
        for dy, dz in OFFSETS:
            chip = (y + dy) % 4 * 8 + (z + dz) % 4 * 2
            send(other, chip, row_there, 1, kind_there)
            send(other, chip + 1, row_there, 1, kind_there)

    def wait_for(count, sem):
        rows = win.at[pl.ds(0, count)]
        pltpu.make_async_copy(rows, rows, sem).wait()

    start = rng[0, tile]
    two = rng[1, tile] > 1

    within = lax.broadcasted_iota(jnp.int32, (8, 128), 1) < 2 + start

    def prepare(group, inside=None):
        w = win[8 * group:8 * group + 8].astype(F32)
        left, right = w[:, 0, :], w[:, 1, :]
        if inside is not None:
            left, right = jnp.where(inside, left, 0.0), jnp.where(inside, right, 0.0)
        rows = slice(8 * group, 8 * group + 8)
        left = pltpu.roll(left, SPAN - 381, 1)
        spun = [pltpu.roll(right[:, 128 * i:128 * i + 128], 2 + start, 1) for i in range(6)]
        right = jnp.concatenate([jnp.where(within, a, b) for a, b in zip(spun, spun[1:])], 1)
        for ref, sums, x, cols in ((lj, lsum, left, 256), (rj, rsum, right, 512)):
            total = square = 0.0
            for j in range(7):
                v = (pltpu.roll(x, x.shape[1] - j, 1) if j else x)[:, :cols]
                ref[j, rows, :] = v
                total, square = total + v, square + v * v
            sums[0, rows, :] = total
            sums[1, rows, :] = square

    sub = lax.broadcasted_iota(jnp.int32, (8, SPAN), 0)
    halo_rows = ((sub < 3) & (band < bands - 1)) | ((sub >= 5) & (band > 0))

    def wait_halo():
        @pl.when(band > 0)
        def _():
            wait_for(3, recv_sem.at[4])

        @pl.when(band < bands - 1)
        def _():
            wait_for(3, recv_sem.at[5])


    upper = lax.broadcasted_iota(jnp.int32, (128, 128), 1) >= lax.broadcasted_iota(jnp.int32, (128, 128), 0)

    def operands(trio):
        wraps = len(trio) == 3

        def box(sums, i, cols):
            h = joined(sums, trio, i)
            near = h[0:8]
            for k in range(1, 7):
                near = near + h[k:k + 8]
            if not wraps:
                return near
            far = h[8:16]
            for k in range(1, 7):
                far = far + h[8 + k:16 + k]
            return jnp.where(sub[:, :cols] >= 5, far, near)

        def stats(sums, cols):
            total = box(sums, 0, cols)
            mean = total * (1.0 / 49.0)
            spread = jnp.maximum(box(sums, 1, cols) * (1.0 / 49.0) - mean * mean, 0.01)
            return total, mean, lax.rsqrt(spread)

        total_l, _, scale_l = stats(lsum, 256)
        _, mean_r, scale_r = stats(rsum, 512)
        a, b = split3(-total_l), split3(mean_r)
        rt = jnp.concatenate([joined(rj, trio, j) for j in range(7)] + [b[q] for _, q in PAIRS], 0).astype(BF16)
        lt = jnp.concatenate([joined(lj, trio, j) for j in range(7)] + [a[p] for p, _ in PAIRS], 0).T.astype(BF16)
        return 8 * len(trio), lt, rt, scale_l * (1.0 / 49.0), scale_r

    def block(step, taps, lt, rt, scale_l, scale_r):
        lane = lax.broadcasted_iota(jnp.int32, (1, lt.shape[1]), 1)
        place = jnp.where(lane < 7 * taps, lane % taps, 100 + (lane - 7 * taps) % 8)
        for k in range(8):
            first = k + (8 if taps == 24 and k >= 5 else 0)
            keep = ((place >= first) & (place <= first + 6)) | (place == 100 + k)
            g = jnp.dot(lt * keep.astype(F32).astype(BF16), rt, preferred_element_type=F32)
            for half in range(2):
                rows = slice(128 * half, 128 * half + 128)
                part = [slice(128 * (half + i), 128 * (half + i + 1)) for i in range(3)]
                s = [g[rows, c] * scale_r[k:k + 1, c] for c in part]
                one, more = jnp.where(upper, s[1], s[2]), jnp.where(upper, s[0], s[1])
                v = jnp.where(two, jnp.maximum(one, more), one)
                v = v.T
                top = v[0:8]
                for q in range(8, 128, 8):
                    top = jnp.maximum(top, v[q:q + 8])
                tops[8 * step + k, :, rows] = top

    wait_for(8, recv_sem.at[0])
    prepare(0)
    wait_for(8, recv_sem.at[1])
    prepare(1)
    wait_for(8, recv_sem.at[2])
    prepare(2)
    wait_for(8, recv_sem.at[3])
    prepare(3)
    parts = [operands((0, 1))]
    parts.append(operands((1, 2)))
    parts.append(operands((2, 3)))
    block(0, *parts[0])
    block(1, *parts[1])
    wait_halo()
    prepare(4, halo_rows)
    parts.append(operands((3, 4, 0)))
    block(2, *parts[2])
    block(3, *parts[3])
    best = jnp.max(tops[...], axis=1) * jnp.concatenate([p[3] for p in parts], 0)
    best_ref[...] = pltpu.roll(best, 3, 0)

    wait_for(tiles - 1, send_sem.at[0])

    @pl.when(crosses)
    def _():
        wait_for(tiles, send_sem.at[1])


def solution(mesh):
    def on_device(left_image, right_image, ranges):
        arrays = [pltpu.with_memory_space_constraint(x, pltpu.HBM) for x in (ranges.T, left_image, right_image)]
        best = pl.pallas_call(
            kernel,
            out_shape=jax.ShapeDtypeStruct((32, 256), F32),
            in_specs=[pl.BlockSpec(memory_space=pltpu.HBM)] * 3,
            out_specs=pl.BlockSpec(memory_space=pltpu.VMEM),
            scratch_shapes=[
                pltpu.SMEM((2, 32), jnp.int32),
                pltpu.VMEM(left_image.shape, BF16),
                pltpu.VMEM(right_image.shape, BF16),
                pltpu.VMEM((2, left_image.shape[1] + 2 * PAD), BF16),
                pltpu.VMEM((40, 2, SPAN), BF16),
                pltpu.VMEM((7, 40, 256), F32),
                pltpu.VMEM((7, 40, 512), F32),
                pltpu.VMEM((2, 40, 256), F32),
                pltpu.VMEM((2, 40, 512), F32),
                pltpu.VMEM((32, 8, 256), F32),
                pltpu.SemaphoreType.DMA((3,)),
                pltpu.SemaphoreType.DMA((2,)),
                pltpu.SemaphoreType.DMA((6,)),
                pltpu.SemaphoreType.REGULAR,
            ],
            name="match",
            compiler_params=pltpu.CompilerParams(collective_id=0, has_side_effects=True, vmem_limit_bytes=16 << 20),
        )(*arrays)
        return jnp.maximum(best, -2.0)

    return jax.shard_map(
        on_device,
        mesh=mesh,
        in_specs=(P(("rows", "cols"), None), P(("rows", "cols"), None), P()),
        out_specs=P("rows", "cols"),
        check_vma=False,
    )
```

```python
import jax
import jax.numpy as jnp
from jax import lax
from jax.experimental import pallas as pl
from jax.experimental.pallas import tpu as pltpu
from jax.sharding import PartitionSpec as P

F32, BF16 = jnp.float32, jnp.bfloat16
SPAN = 768
PAD = 384
MESH = pl.DeviceIdType.MESH
OFFSETS = sorted(((dy, dz) for dy in range(4) for dz in range(4)), key=lambda o: -(2 - abs(o[0] - 2)) - (2 - abs(o[1] - 2)))
PAIRS = ((0, 0), (0, 1), (1, 0), (1, 1), (0, 2), (2, 0))


def split3(x):
    hi = x.astype(BF16).astype(F32)
    mid = (x - hi).astype(BF16).astype(F32)
    return hi, mid, (x - hi) - mid


def joined(ref, tiles, *lead):
    return jnp.concatenate([ref[(*lead, slice(8 * t, 8 * t + 8), slice(None))] for t in tiles], 0)


def kernel(rng_hbm, l_hbm, r_hbm, best_ref, rng, l_row, r_row, stage, win, lj, rj, lsum, rsum, tops,
           load_sem, send_sem, recv_sem, go):
    band, tile = lax.axis_index("rows"), lax.axis_index("cols")
    bands, tiles = lax.axis_size("rows"), lax.axis_size("cols")
    width = l_hbm.shape[1]
    y, z, core = tile // 8, tile // 2 % 4, tile % 2
    goes_up = (tile < 3) & (band > 0)
    goes_down = (tile >= tiles - 3) & (band < bands - 1)
    other = jnp.where(goes_up, band - 1, band + 1)
    crosses = goes_up | goes_down
    asked = ((tile < 3) & (band < bands - 1)) | ((tile >= tiles - 3) & (band > 0))
    asker = jnp.where(tile < 3, band + 1, band - 1)
    barrier = pltpu.get_barrier_semaphore()

    loads = [pltpu.make_async_copy(a, b, load_sem.at[k])
             for k, (a, b) in enumerate(((l_hbm, l_row), (r_hbm, r_row), (rng_hbm, rng)))]

    def greet(other_band, other_tile):
        pl.semaphore_signal(barrier, inc=1, device_id=(other_band, other_tile), device_id_type=MESH)

    def peers(dy, dz):
        chip = (y + dy) % 4 * 8 + (z + dz) % 4 * 2
        return [chip + 1 - core] + ([chip + core] if dy or dz else [])

    @pl.when(crosses)
    def _():
        greet(other, tile)

    for dy, dz in OFFSETS:
        for peer in peers(dy, dz):
            greet(band, peer)

    for load in loads:
        load.start()
    for load in loads:
        load.wait()
    stage[:, :PAD] = jnp.zeros((2, PAD), stage.dtype)
    stage[:, PAD + width:] = jnp.zeros((2, PAD), stage.dtype)
    stage[0:1, PAD:PAD + width] = l_row[...]
    stage[1:2, PAD:PAD + width] = r_row[...]

    def window(peer):
        return stage.at[:, pl.ds(pl.multiple_of(peer * 256, 256), SPAN)]

    def send(other_band, peer, row, slot, kind):
        pltpu.make_async_remote_copy(
            src_ref=window(peer), dst_ref=win.at[row], send_sem=send_sem.at[slot], recv_sem=recv_sem.at[kind],
            device_id=(other_band, peer), device_id_type=MESH).start()

    pltpu.make_async_copy(window(tile), win.at[tile], recv_sem.at[y]).start()
    pl.semaphore_wait(barrier, tiles - 1 + asked.astype(jnp.int32))

    @pl.when(asked)
    def _():
        pl.semaphore_signal(go, inc=1, device_id=(asker, tile), device_id_type=MESH)

    row_there = jnp.where(goes_up, tiles + tile, tile + 8)
    kind_there = jnp.where(goes_up, 5, 4)
    for dy, dz in OFFSETS:
        for peer in peers(dy, dz):
            send(band, peer, tile, 0, y)

    @pl.when(crosses)
    def _():
        pl.semaphore_wait(go, 1)
        for dy, dz in OFFSETS:
            chip = (y + dy) % 4 * 8 + (z + dz) % 4 * 2
            send(other, chip, row_there, 1, kind_there)
            send(other, chip + 1, row_there, 1, kind_there)

    def wait_for(count, sem):
        rows = win.at[pl.ds(0, count)]
        pltpu.make_async_copy(rows, rows, sem).wait()

    start = rng[0, tile]
    two = rng[1, tile] > 1

    within = lax.broadcasted_iota(jnp.int32, (8, 128), 1) < 2 + start

    def prepare(group, inside=None):
        w = win[8 * group:8 * group + 8].astype(F32)
        left, right = w[:, 0, :], w[:, 1, :]
        if inside is not None:
            left, right = jnp.where(inside, left, 0.0), jnp.where(inside, right, 0.0)
        rows = slice(8 * group, 8 * group + 8)
        left = pltpu.roll(left, SPAN - 381, 1)
        spun = [pltpu.roll(right[:, 128 * i:128 * i + 128], 2 + start, 1) for i in range(6)]
        right = jnp.concatenate([jnp.where(within, a, b) for a, b in zip(spun, spun[1:])], 1)
        for ref, sums, x, cols in ((lj, lsum, left, 256), (rj, rsum, right, 512)):
            total = square = 0.0
            for j in range(7):
                v = (pltpu.roll(x, x.shape[1] - j, 1) if j else x)[:, :cols]
                ref[j, rows, :] = v
                total, square = total + v, square + v * v
            sums[0, rows, :] = total
            sums[1, rows, :] = square

    sub = lax.broadcasted_iota(jnp.int32, (8, SPAN), 0)
    halo_rows = ((sub < 3) & (band < bands - 1)) | ((sub >= 5) & (band > 0))

    def wait_halo():
        @pl.when(band > 0)
        def _():
            wait_for(3, recv_sem.at[4])

        @pl.when(band < bands - 1)
        def _():
            wait_for(3, recv_sem.at[5])


    upper = lax.broadcasted_iota(jnp.int32, (128, 128), 1) >= lax.broadcasted_iota(jnp.int32, (128, 128), 0)

    def operands(trio):
        wraps = len(trio) == 3

        def box(sums, i, cols):
            h = joined(sums, trio, i)
            near = h[0:8]
            for k in range(1, 7):
                near = near + h[k:k + 8]
            if not wraps:
                return near
            far = h[8:16]
            for k in range(1, 7):
                far = far + h[8 + k:16 + k]
            return jnp.where(sub[:, :cols] >= 5, far, near)

        def stats(sums, cols):
            total = box(sums, 0, cols)
            mean = total * (1.0 / 49.0)
            spread = jnp.maximum(box(sums, 1, cols) * (1.0 / 49.0) - mean * mean, 0.01)
            return total, mean, lax.rsqrt(spread)

        total_l, _, scale_l = stats(lsum, 256)
        _, mean_r, scale_r = stats(rsum, 512)
        a, b = split3(-total_l), split3(mean_r)
        rt = jnp.concatenate([joined(rj, trio, j) for j in range(7)] + [b[q] for _, q in PAIRS], 0).astype(BF16)
        lt = jnp.concatenate([joined(lj, trio, j) for j in range(7)] + [a[p] for p, _ in PAIRS], 0).T.astype(BF16)
        return 8 * len(trio), lt, rt, scale_l * (1.0 / 49.0), scale_r

    def block(step, taps, lt, rt, scale_l, scale_r):
        lane = lax.broadcasted_iota(jnp.int32, (1, lt.shape[1]), 1)
        place = jnp.where(lane < 7 * taps, lane % taps, 100 + (lane - 7 * taps) % 8)
        for k in range(8):
            first = k + (8 if taps == 24 and k >= 5 else 0)
            keep = ((place >= first) & (place <= first + 6)) | (place == 100 + k)
            g = jnp.dot(lt * keep.astype(F32).astype(BF16), rt, preferred_element_type=F32)
            for half in range(2):
                rows = slice(128 * half, 128 * half + 128)
                part = [slice(128 * (half + i), 128 * (half + i + 1)) for i in range(3)]
                s = [g[rows, c] * scale_r[k:k + 1, c] for c in part]
                one, more = jnp.where(upper, s[1], s[2]), jnp.where(upper, s[0], s[1])
                v = jnp.where(two, jnp.maximum(one, more), one)
                v = v.T
                top = v[0:8]
                for q in range(8, 128, 8):
                    top = jnp.maximum(top, v[q:q + 8])
                tops[8 * step + k, :, rows] = top

    wait_for(8, recv_sem.at[0])
    prepare(0)
    wait_for(8, recv_sem.at[1])
    prepare(1)
    wait_for(8, recv_sem.at[2])
    wait_for(8, recv_sem.at[3])
    prepare(2)
    prepare(3)
    parts = [operands((0, 1))]
    parts.append(operands((1, 2)))
    parts.append(operands((2, 3)))
    block(0, *parts[0])
    block(1, *parts[1])
    wait_halo()
    prepare(4, halo_rows)
    parts.append(operands((3, 4, 0)))
    block(2, *parts[2])
    block(3, *parts[3])
    best = jnp.max(tops[...], axis=1) * jnp.concatenate([p[3] for p in parts], 0)
    best_ref[...] = pltpu.roll(best, 3, 0)

    wait_for(tiles - 1, send_sem.at[0])

    @pl.when(crosses)
    def _():
        wait_for(tiles, send_sem.at[1])


def solution(mesh):
    def on_device(left_image, right_image, ranges):
        arrays = [pltpu.with_memory_space_constraint(x, pltpu.HBM) for x in (ranges.T, left_image, right_image)]
        best = pl.pallas_call(
            kernel,
            out_shape=jax.ShapeDtypeStruct((32, 256), F32),
            in_specs=[pl.BlockSpec(memory_space=pltpu.HBM)] * 3,
            out_specs=pl.BlockSpec(memory_space=pltpu.VMEM),
            scratch_shapes=[
                pltpu.SMEM((2, 32), jnp.int32),
                pltpu.VMEM(left_image.shape, BF16),
                pltpu.VMEM(right_image.shape, BF16),
                pltpu.VMEM((2, left_image.shape[1] + 2 * PAD), BF16),
                pltpu.VMEM((40, 2, SPAN), BF16),
                pltpu.VMEM((7, 40, 256), F32),
                pltpu.VMEM((7, 40, 512), F32),
                pltpu.VMEM((2, 40, 256), F32),
                pltpu.VMEM((2, 40, 512), F32),
                pltpu.VMEM((32, 8, 256), F32),
                pltpu.SemaphoreType.DMA((3,)),
                pltpu.SemaphoreType.DMA((2,)),
                pltpu.SemaphoreType.DMA((6,)),
                pltpu.SemaphoreType.REGULAR,
            ],
            name="match",
            compiler_params=pltpu.CompilerParams(collective_id=0, has_side_effects=True, vmem_limit_bytes=16 << 20),
        )(*arrays)
        return jnp.maximum(best, -2.0)

    return jax.shard_map(
        on_device,
        mesh=mesh,
        in_specs=(P(("rows", "cols"), None), P(("rows", "cols"), None), P()),
        out_specs=P("rows", "cols"),
        check_vma=False,
    )
```

```python
import jax
import jax.numpy as jnp
from jax import lax
from jax.experimental import pallas as pl
from jax.experimental.pallas import tpu as pltpu
from jax.sharding import PartitionSpec as P

F32, BF16 = jnp.float32, jnp.bfloat16
SPAN = 640
PAD = 381
MESH = pl.DeviceIdType.MESH
OFFSETS = sorted(((dy, dz) for dy in range(4) for dz in range(4)), key=lambda o: -(2 - abs(o[0] - 2)) - (2 - abs(o[1] - 2)))
PAIRS = ((0, 0), (0, 1), (1, 0), (1, 1), (0, 2), (2, 0))


def split3(x):
    hi = x.astype(BF16).astype(F32)
    mid = (x - hi).astype(BF16).astype(F32)
    return hi, mid, (x - hi) - mid


def joined(ref, tiles, *lead):
    return jnp.concatenate([ref[(*lead, slice(8 * t, 8 * t + 8), slice(None))] for t in tiles], 0)


def kernel(rng_hbm, l_hbm, r_hbm, best_ref, rng, l_row, r_row, stage, win, lj, rj, lsum, rsum, tops,
           load_sem, send_sem, recv_sem, go):
    band, tile = lax.axis_index("rows"), lax.axis_index("cols")
    bands, tiles = lax.axis_size("rows"), lax.axis_size("cols")
    width = l_hbm.shape[1]
    y, z, core = tile // 8, tile // 2 % 4, tile % 2
    goes_up = (tile < 3) & (band > 0)
    goes_down = (tile >= tiles - 3) & (band < bands - 1)
    other = jnp.where(goes_up, band - 1, band + 1)
    crosses = goes_up | goes_down
    asked = ((tile < 3) & (band < bands - 1)) | ((tile >= tiles - 3) & (band > 0))
    asker = jnp.where(tile < 3, band + 1, band - 1)
    barrier = pltpu.get_barrier_semaphore()

    loads = [pltpu.make_async_copy(a, b, load_sem.at[k])
             for k, (a, b) in enumerate(((l_hbm, l_row), (r_hbm, r_row), (rng_hbm, rng)))]

    def greet(other_band, other_tile):
        pl.semaphore_signal(barrier, inc=1, device_id=(other_band, other_tile), device_id_type=MESH)

    def peers(dy, dz):
        chip = (y + dy) % 4 * 8 + (z + dz) % 4 * 2
        return [chip + 1 - core] + ([chip + core] if dy or dz else [])

    @pl.when(crosses)
    def _():
        greet(other, tile)

    for dy, dz in OFFSETS:
        for peer in peers(dy, dz):
            greet(band, peer)

    for load in loads:
        load.start()
    for load in loads:
        load.wait()
    stage[:, :384] = jnp.zeros((2, 384), stage.dtype)
    stage[:, width + 256:] = jnp.zeros((2, 128), stage.dtype)
    stage[0:1, PAD:PAD + width] = l_row[...]
    stage[1:2, PAD:PAD + width] = r_row[...]

    def window(peer):
        return stage.at[:, pl.ds(pl.multiple_of(peer * 256, 256), SPAN)]

    def send(other_band, peer, row, slot, kind):
        pltpu.make_async_remote_copy(
            src_ref=window(peer), dst_ref=win.at[row], send_sem=send_sem.at[slot], recv_sem=recv_sem.at[kind],
            device_id=(other_band, peer), device_id_type=MESH).start()

    pltpu.make_async_copy(window(tile), win.at[tile], recv_sem.at[y]).start()
    pl.semaphore_wait(barrier, tiles - 1 + asked.astype(jnp.int32))

    @pl.when(asked)
    def _():
        pl.semaphore_signal(go, inc=1, device_id=(asker, tile), device_id_type=MESH)

    row_there = jnp.where(goes_up, tiles + tile, tile + 8)
    kind_there = jnp.where(goes_up, 5, 4)
    for dy, dz in OFFSETS:
        for peer in peers(dy, dz):
            send(band, peer, tile, 0, y)

    @pl.when(crosses)
    def _():
        pl.semaphore_wait(go, 1)
        for dy, dz in OFFSETS:
            chip = (y + dy) % 4 * 8 + (z + dz) % 4 * 2
            send(other, chip, row_there, 1, kind_there)
            send(other, chip + 1, row_there, 1, kind_there)

    def wait_for(count, sem):
        rows = win.at[pl.ds(0, count)]
        pltpu.make_async_copy(rows, rows, sem).wait()

    start = rng[0, tile]
    two = rng[1, tile] > 1

    within = lax.broadcasted_iota(jnp.int32, (8, 128), 1) < 5 + start

    def prepare(group, inside=None):
        w = win[8 * group:8 * group + 8].astype(F32)
        left, right = w[:, 0, :], w[:, 1, :]
        if inside is not None:
            left, right = jnp.where(inside, left, 0.0), jnp.where(inside, right, 0.0)
        rows = slice(8 * group, 8 * group + 8)
        left = pltpu.roll(left[:, 256:], 384 - 122, 1)
        spun = [pltpu.roll(right[:, 128 * i:128 * i + 128], 5 + start, 1) for i in range(5)]
        right = jnp.concatenate([jnp.where(within, a, b) for a, b in zip(spun, spun[1:] + spun[:1])], 1)
        for ref, sums, x, cols in ((lj, lsum, left, 256), (rj, rsum, right, 512)):
            total = square = 0.0
            for j in range(7):
                v = (pltpu.roll(x, x.shape[1] - j, 1) if j else x)[:, :cols]
                ref[j, rows, :] = v
                total, square = total + v, square + v * v
            sums[0, rows, :] = total
            sums[1, rows, :] = square

    sub = lax.broadcasted_iota(jnp.int32, (8, SPAN), 0)
    halo_rows = ((sub < 3) & (band < bands - 1)) | ((sub >= 5) & (band > 0))

    def wait_halo():
        @pl.when(band > 0)
        def _():
            wait_for(3, recv_sem.at[4])

        @pl.when(band < bands - 1)
        def _():
            wait_for(3, recv_sem.at[5])


    upper = lax.broadcasted_iota(jnp.int32, (128, 128), 1) >= lax.broadcasted_iota(jnp.int32, (128, 128), 0)

    def operands(trio):
        wraps = len(trio) == 3

        def box(sums, i, cols):
            h = joined(sums, trio, i)
            near = h[0:8]
            for k in range(1, 7):
                near = near + h[k:k + 8]
            if not wraps:
                return near
            far = h[8:16]
            for k in range(1, 7):
                far = far + h[8 + k:16 + k]
            return jnp.where(sub[:, :cols] >= 5, far, near)

        def stats(sums, cols):
            total = box(sums, 0, cols)
            mean = total * (1.0 / 49.0)
            spread = jnp.maximum(box(sums, 1, cols) * (1.0 / 49.0) - mean * mean, 0.01)
            return total, mean, lax.rsqrt(spread)

        total_l, _, scale_l = stats(lsum, 256)
        _, mean_r, scale_r = stats(rsum, 512)
        a, b = split3(-total_l), split3(mean_r)
        rt = jnp.concatenate([joined(rj, trio, j) for j in range(7)] + [b[q] for _, q in PAIRS], 0).astype(BF16)
        lt = jnp.concatenate([joined(lj, trio, j) for j in range(7)] + [a[p] for p, _ in PAIRS], 0).T.astype(BF16)
        return 8 * len(trio), lt, rt, scale_l * (1.0 / 49.0), scale_r

    def block(step, taps, lt, rt, scale_l, scale_r):
        lane = lax.broadcasted_iota(jnp.int32, (1, lt.shape[1]), 1)
        place = jnp.where(lane < 7 * taps, lane % taps, 100 + (lane - 7 * taps) % 8)
        for k in range(8):
            first = k + (8 if taps == 24 and k >= 5 else 0)
            keep = ((place >= first) & (place <= first + 6)) | (place == 100 + k)
            g = jnp.dot(lt * keep.astype(F32).astype(BF16), rt, preferred_element_type=F32)
            for half in range(2):
                rows = slice(128 * half, 128 * half + 128)
                part = [slice(128 * (half + i), 128 * (half + i + 1)) for i in range(3)]
                s = [g[rows, c] * scale_r[k:k + 1, c] for c in part]
                one, more = jnp.where(upper, s[1], s[2]), jnp.where(upper, s[0], s[1])
                v = jnp.where(two, jnp.maximum(one, more), one)
                v = v.T
                top = v[0:8]
                for q in range(8, 128, 8):
                    top = jnp.maximum(top, v[q:q + 8])
                tops[8 * step + k, :, rows] = top

    wait_for(8, recv_sem.at[0])
    prepare(0)
    wait_for(8, recv_sem.at[1])
    prepare(1)
    wait_for(8, recv_sem.at[2])
    wait_for(8, recv_sem.at[3])
    prepare(2)
    prepare(3)
    parts = [operands((0, 1))]
    parts.append(operands((1, 2)))
    parts.append(operands((2, 3)))
    block(0, *parts[0])
    block(1, *parts[1])
    wait_halo()
    prepare(4, halo_rows)
    parts.append(operands((3, 4, 0)))
    block(2, *parts[2])
    block(3, *parts[3])
    best = jnp.max(tops[...], axis=1) * jnp.concatenate([p[3] for p in parts], 0)
    best_ref[...] = pltpu.roll(best, 3, 0)

    wait_for(tiles - 1, send_sem.at[0])

    @pl.when(crosses)
    def _():
        wait_for(tiles, send_sem.at[1])


def solution(mesh):
    def on_device(left_image, right_image, ranges):
        arrays = [pltpu.with_memory_space_constraint(x, pltpu.HBM) for x in (ranges.T, left_image, right_image)]
        best = pl.pallas_call(
            kernel,
            out_shape=jax.ShapeDtypeStruct((32, 256), F32),
            in_specs=[pl.BlockSpec(memory_space=pltpu.HBM)] * 3,
            out_specs=pl.BlockSpec(memory_space=pltpu.VMEM),
            scratch_shapes=[
                pltpu.SMEM((2, 32), jnp.int32),
                pltpu.VMEM(left_image.shape, BF16),
                pltpu.VMEM(right_image.shape, BF16),
                pltpu.VMEM((2, left_image.shape[1] + 384), BF16),
                pltpu.VMEM((40, 2, SPAN), BF16),
                pltpu.VMEM((7, 40, 256), F32),
                pltpu.VMEM((7, 40, 512), F32),
                pltpu.VMEM((2, 40, 256), F32),
                pltpu.VMEM((2, 40, 512), F32),
                pltpu.VMEM((32, 8, 256), F32),
                pltpu.SemaphoreType.DMA((3,)),
                pltpu.SemaphoreType.DMA((2,)),
                pltpu.SemaphoreType.DMA((6,)),
                pltpu.SemaphoreType.REGULAR,
            ],
            name="match",
            compiler_params=pltpu.CompilerParams(collective_id=0, has_side_effects=True, vmem_limit_bytes=16 << 20),
        )(*arrays)
        return jnp.maximum(best, -2.0)

    return jax.shard_map(
        on_device,
        mesh=mesh,
        in_specs=(P(("rows", "cols"), None), P(("rows", "cols"), None), P()),
        out_specs=P("rows", "cols"),
        check_vma=False,
    )
```

```python
import jax
import jax.numpy as jnp
from jax import lax
from jax.experimental import pallas as pl
from jax.experimental.pallas import tpu as pltpu
from jax.sharding import PartitionSpec as P

F32, BF16 = jnp.float32, jnp.bfloat16
SPAN = 768
PAD = 384
MESH = pl.DeviceIdType.MESH
OFFSETS = sorted(((dy, dz) for dy in range(4) for dz in range(4)), key=lambda o: -(2 - abs(o[0] - 2)) - (2 - abs(o[1] - 2)))
PAIRS = ((0, 0), (0, 1), (1, 0), (1, 1), (0, 2), (2, 0))


def split3(x):
    hi = x.astype(BF16).astype(F32)
    mid = (x - hi).astype(BF16).astype(F32)
    return hi, mid, (x - hi) - mid


def joined(ref, tiles, *lead):
    return jnp.concatenate([ref[(*lead, slice(8 * t, 8 * t + 8), slice(None))] for t in tiles], 0)


def kernel(rng_hbm, l_hbm, r_hbm, best_ref, rng, l_row, r_row, stage, win, lj, rj, lsum, rsum, tops,
           load_sem, send_sem, recv_sem, go):
    band, tile = lax.axis_index("rows"), lax.axis_index("cols")
    bands, tiles = lax.axis_size("rows"), lax.axis_size("cols")
    width = l_hbm.shape[1]
    y, z, core = tile // 8, tile // 2 % 4, tile % 2
    goes_up = (tile < 3) & (band > 0)
    goes_down = (tile >= tiles - 3) & (band < bands - 1)
    other = jnp.where(goes_up, band - 1, band + 1)
    crosses = goes_up | goes_down
    asked = ((tile < 3) & (band < bands - 1)) | ((tile >= tiles - 3) & (band > 0))
    asker = jnp.where(tile < 3, band + 1, band - 1)
    barrier = pltpu.get_barrier_semaphore()

    loads = [pltpu.make_async_copy(a, b, load_sem.at[k])
             for k, (a, b) in enumerate(((l_hbm, l_row), (r_hbm, r_row), (rng_hbm, rng)))]

    def greet(other_band, other_tile):
        pl.semaphore_signal(barrier, inc=1, device_id=(other_band, other_tile), device_id_type=MESH)

    def peers(dy, dz):
        chip = (y + dy) % 4 * 8 + (z + dz) % 4 * 2
        return [chip + 1 - core] + ([chip + core] if dy or dz else [])

    @pl.when(crosses)
    def _():
        greet(other, tile)

    for dy, dz in OFFSETS:
        for peer in peers(dy, dz):
            greet(band, peer)

    for load in loads:
        load.start()
    for load in loads:
        load.wait()
    stage[:, :PAD] = jnp.zeros((2, PAD), stage.dtype)
    stage[:, PAD + width:] = jnp.zeros((2, PAD), stage.dtype)
    stage[0:1, PAD:PAD + width] = l_row[...]
    stage[1:2, PAD:PAD + width] = r_row[...]

    def window(peer):
        return stage.at[:, pl.ds(pl.multiple_of(peer * 256, 256), SPAN)]

    def send(other_band, peer, row, slot, kind):
        pltpu.make_async_remote_copy(
            src_ref=window(peer), dst_ref=win.at[row], send_sem=send_sem.at[slot], recv_sem=recv_sem.at[kind],
            device_id=(other_band, peer), device_id_type=MESH).start()

    pltpu.make_async_copy(window(tile), win.at[tile], recv_sem.at[y]).start()
    pl.semaphore_wait(barrier, tiles - 1 + asked.astype(jnp.int32))

    @pl.when(asked)
    def _():
        pl.semaphore_signal(go, inc=1, device_id=(asker, tile), device_id_type=MESH)

    row_there = jnp.where(goes_up, tiles + tile, tile + 8)
    kind_there = jnp.where(goes_up, 5, 4)
    for dy, dz in OFFSETS:
        for peer in peers(dy, dz):
            send(band, peer, tile, 0, y)

    @pl.when(crosses)
    def _():
        pl.semaphore_wait(go, 1)
        for dy, dz in OFFSETS:
            chip = (y + dy) % 4 * 8 + (z + dz) % 4 * 2
            send(other, chip, row_there, 1, kind_there)
            send(other, chip + 1, row_there, 1, kind_there)

    def wait_for(count, sem):
        rows = win.at[pl.ds(0, count)]
        pltpu.make_async_copy(rows, rows, sem).wait()

    start = rng[0, tile]
    two = rng[1, tile] > 1

    within = lax.broadcasted_iota(jnp.int32, (8, 128), 1) < 2 + start

    def prepare(group, inside=None):
        w = win[8 * group:8 * group + 8].astype(F32)
        left, right = w[:, 0, :], w[:, 1, :]
        if inside is not None:
            left, right = jnp.where(inside, left, 0.0), jnp.where(inside, right, 0.0)
        rows = slice(8 * group, 8 * group + 8)
        left = pltpu.roll(left[:, 256:], 512 - 125, 1)[:, :384]
        spun = [pltpu.roll(right[:, 128 * i:128 * i + 128], 2 + start, 1) for i in range(6)]
        right = jnp.concatenate([jnp.where(within, a, b) for a, b in zip(spun, spun[1:])], 1)
        for ref, sums, x, cols in ((lj, lsum, left, 256), (rj, rsum, right, 512)):
            total = square = 0.0
            for j in range(7):
                v = (pltpu.roll(x, x.shape[1] - j, 1) if j else x)[:, :cols]
                ref[j, rows, :] = v
                total, square = total + v, square + v * v
            sums[0, rows, :] = total
            sums[1, rows, :] = square

    sub = lax.broadcasted_iota(jnp.int32, (8, SPAN), 0)
    halo_rows = ((sub < 3) & (band < bands - 1)) | ((sub >= 5) & (band > 0))

    def wait_halo():
        @pl.when(band > 0)
        def _():
            wait_for(3, recv_sem.at[4])

        @pl.when(band < bands - 1)
        def _():
            wait_for(3, recv_sem.at[5])


    upper = lax.broadcasted_iota(jnp.int32, (128, 128), 1) >= lax.broadcasted_iota(jnp.int32, (128, 128), 0)

    def operands(trio):
        wraps = len(trio) == 3

        def box(sums, i, cols):
            h = joined(sums, trio, i)
            near = h[0:8]
            for k in range(1, 7):
                near = near + h[k:k + 8]
            if not wraps:
                return near
            far = h[8:16]
            for k in range(1, 7):
                far = far + h[8 + k:16 + k]
            return jnp.where(sub[:, :cols] >= 5, far, near)

        def stats(sums, cols):
            total = box(sums, 0, cols)
            mean = total * (1.0 / 49.0)
            spread = jnp.maximum(box(sums, 1, cols) * (1.0 / 49.0) - mean * mean, 0.01)
            return total, mean, lax.rsqrt(spread)

        total_l, _, scale_l = stats(lsum, 256)
        _, mean_r, scale_r = stats(rsum, 512)
        a, b = split3(-total_l), split3(mean_r)
        rt = jnp.concatenate([joined(rj, trio, j) for j in range(7)] + [b[q] for _, q in PAIRS], 0).astype(BF16)
        lt = jnp.concatenate([joined(lj, trio, j) for j in range(7)] + [a[p] for p, _ in PAIRS], 0).T.astype(BF16)
        return 8 * len(trio), lt, rt, scale_l * (1.0 / 49.0), scale_r

    def block(step, taps, lt, rt, scale_l, scale_r):
        lane = lax.broadcasted_iota(jnp.int32, (1, lt.shape[1]), 1)
        place = jnp.where(lane < 7 * taps, lane % taps, 100 + (lane - 7 * taps) % 8)
        for k in range(8):
            first = k + (8 if taps == 24 and k >= 5 else 0)
            keep = ((place >= first) & (place <= first + 6)) | (place == 100 + k)
            g = jnp.dot(lt * keep.astype(F32).astype(BF16), rt, preferred_element_type=F32)
            for half in range(2):
                rows = slice(128 * half, 128 * half + 128)
                part = [slice(128 * (half + i), 128 * (half + i + 1)) for i in range(3)]
                s = [g[rows, c] * scale_r[k:k + 1, c] for c in part]
                one, more = jnp.where(upper, s[1], s[2]), jnp.where(upper, s[0], s[1])
                v = jnp.where(two, jnp.maximum(one, more), one)
                v = v.T
                top = v[0:8]
                for q in range(8, 128, 8):
                    top = jnp.maximum(top, v[q:q + 8])
                tops[8 * step + k, :, rows] = top

    wait_for(8, recv_sem.at[0])
    prepare(0)
    wait_for(8, recv_sem.at[1])
    prepare(1)
    wait_for(8, recv_sem.at[2])
    wait_for(8, recv_sem.at[3])
    prepare(2)
    prepare(3)
    parts = [operands((0, 1))]
    parts.append(operands((1, 2)))
    parts.append(operands((2, 3)))
    block(0, *parts[0])
    block(1, *parts[1])
    wait_halo()
    prepare(4, halo_rows)
    parts.append(operands((3, 4, 0)))
    block(2, *parts[2])
    block(3, *parts[3])
    best = jnp.max(tops[...], axis=1) * jnp.concatenate([p[3] for p in parts], 0)
    best_ref[...] = pltpu.roll(best, 3, 0)

    wait_for(tiles - 1, send_sem.at[0])

    @pl.when(crosses)
    def _():
        wait_for(tiles, send_sem.at[1])


def solution(mesh):
    def on_device(left_image, right_image, ranges):
        arrays = [pltpu.with_memory_space_constraint(x, pltpu.HBM) for x in (ranges.T, left_image, right_image)]
        best = pl.pallas_call(
            kernel,
            out_shape=jax.ShapeDtypeStruct((32, 256), F32),
            in_specs=[pl.BlockSpec(memory_space=pltpu.HBM)] * 3,
            out_specs=pl.BlockSpec(memory_space=pltpu.VMEM),
            scratch_shapes=[
                pltpu.SMEM((2, 32), jnp.int32),
                pltpu.VMEM(left_image.shape, BF16),
                pltpu.VMEM(right_image.shape, BF16),
                pltpu.VMEM((2, left_image.shape[1] + 2 * PAD), BF16),
                pltpu.VMEM((40, 2, SPAN), BF16),
                pltpu.VMEM((7, 40, 256), F32),
                pltpu.VMEM((7, 40, 512), F32),
                pltpu.VMEM((2, 40, 256), F32),
                pltpu.VMEM((2, 40, 512), F32),
                pltpu.VMEM((32, 8, 256), F32),
                pltpu.SemaphoreType.DMA((3,)),
                pltpu.SemaphoreType.DMA((2,)),
                pltpu.SemaphoreType.DMA((6,)),
                pltpu.SemaphoreType.REGULAR,
            ],
            name="match",
            compiler_params=pltpu.CompilerParams(collective_id=0, has_side_effects=True, vmem_limit_bytes=16 << 20),
        )(*arrays)
        return jnp.maximum(best, -2.0)

    return jax.shard_map(
        on_device,
        mesh=mesh,
        in_specs=(P(("rows", "cols"), None), P(("rows", "cols"), None), P()),
        out_specs=P("rows", "cols"),
        check_vma=False,
    )
```

```python
import jax
import jax.numpy as jnp
from jax import lax
from jax.experimental import pallas as pl
from jax.experimental.pallas import tpu as pltpu
from jax.sharding import PartitionSpec as P

F32, BF16 = jnp.float32, jnp.bfloat16
SPAN = 768
PAD = 384
MESH = pl.DeviceIdType.MESH
OFFSETS = sorted(((dy, dz) for dy in range(4) for dz in range(4)), key=lambda o: -(2 - abs(o[0] - 2)) - (2 - abs(o[1] - 2)))
PAIRS = ((0, 0), (0, 1), (1, 0), (1, 1), (0, 2), (2, 0))


def split3(x):
    hi = x.astype(BF16).astype(F32)
    mid = (x - hi).astype(BF16).astype(F32)
    return hi, mid, (x - hi) - mid


def joined(ref, tiles, *lead):
    return jnp.concatenate([ref[(*lead, slice(8 * t, 8 * t + 8), slice(None))] for t in tiles], 0)


def kernel(rng_hbm, l_hbm, r_hbm, best_ref, rng, l_row, r_row, stage, win, lj, rj, lsum, rsum, tops,
           load_sem, send_sem, recv_sem, go):
    band, tile = lax.axis_index("rows"), lax.axis_index("cols")
    bands, tiles = lax.axis_size("rows"), lax.axis_size("cols")
    width = l_hbm.shape[1]
    y, z, core = tile // 8, tile // 2 % 4, tile % 2
    goes_up = (tile < 3) & (band > 0)
    goes_down = (tile >= tiles - 3) & (band < bands - 1)
    other = jnp.where(goes_up, band - 1, band + 1)
    crosses = goes_up | goes_down
    asked = ((tile < 3) & (band < bands - 1)) | ((tile >= tiles - 3) & (band > 0))
    asker = jnp.where(tile < 3, band + 1, band - 1)
    barrier = pltpu.get_barrier_semaphore()

    loads = [pltpu.make_async_copy(a, b, load_sem.at[k])
             for k, (a, b) in enumerate(((l_hbm, l_row), (r_hbm, r_row), (rng_hbm, rng)))]

    def greet(other_band, other_tile):
        pl.semaphore_signal(barrier, inc=1, device_id=(other_band, other_tile), device_id_type=MESH)

    def peers(dy, dz):
        chip = (y + dy) % 4 * 8 + (z + dz) % 4 * 2
        return [chip + 1 - core] + ([chip + core] if dy or dz else [])

    @pl.when(crosses)
    def _():
        greet(other, tile)

    for dy, dz in OFFSETS:
        for peer in peers(dy, dz):
            greet(band, peer)

    for load in loads:
        load.start()
    for load in loads:
        load.wait()
    stage[:, :PAD] = jnp.zeros((2, PAD), stage.dtype)
    stage[:, PAD + width:] = jnp.zeros((2, PAD), stage.dtype)
    stage[0:1, PAD:PAD + width] = l_row[...]
    stage[1:2, PAD:PAD + width] = r_row[...]

    def window(peer):
        return stage.at[:, pl.ds(pl.multiple_of(peer * 256, 256), SPAN)]

    def send(other_band, peer, row, slot, kind):
        pltpu.make_async_remote_copy(
            src_ref=window(peer), dst_ref=win.at[row], send_sem=send_sem.at[slot], recv_sem=recv_sem.at[kind],
            device_id=(other_band, peer), device_id_type=MESH).start()

    pltpu.make_async_copy(window(tile), win.at[tile], recv_sem.at[y]).start()
    pl.semaphore_wait(barrier, tiles - 1 + asked.astype(jnp.int32))

    @pl.when(asked)
    def _():
        pl.semaphore_signal(go, inc=1, device_id=(asker, tile), device_id_type=MESH)

    row_there = jnp.where(goes_up, tiles + tile, tile + 8)
    kind_there = jnp.where(goes_up, 5, 4)
    for dy, dz in OFFSETS:
        for peer in peers(dy, dz):
            send(band, peer, tile, 0, y)

    @pl.when(crosses)
    def _():
        pl.semaphore_wait(go, 1)
        for dy, dz in OFFSETS:
            chip = (y + dy) % 4 * 8 + (z + dz) % 4 * 2
            send(other, chip, row_there, 1, kind_there)
            send(other, chip + 1, row_there, 1, kind_there)

    def wait_for(count, sem):
        rows = win.at[pl.ds(0, count)]
        pltpu.make_async_copy(rows, rows, sem).wait()

    start = rng[0, tile]
    two = rng[1, tile] > 1

    within = lax.broadcasted_iota(jnp.int32, (8, 128), 1) < 2 + start

    def prepare(group, inside=None):
        w = win[8 * group:8 * group + 8].astype(F32)
        left, right = w[:, 0, :], w[:, 1, :]
        if inside is not None:
            left, right = jnp.where(inside, left, 0.0), jnp.where(inside, right, 0.0)
        rows = slice(8 * group, 8 * group + 8)
        left = pltpu.roll(left[:, 256:], 512 - 125, 1)[:, :384]
        spun = [pltpu.roll(right[:, 128 * i:128 * i + 128], 2 + start, 1) for i in range(6)]
        right = jnp.concatenate([jnp.where(within, a, b) for a, b in zip(spun, spun[1:])], 1)
        for ref, sums, x, cols in ((lj, lsum, left, 256), (rj, rsum, right, 512)):
            total = square = 0.0
            for j in range(7):
                v = (pltpu.roll(x, x.shape[1] - j, 1) if j else x)[:, :cols]
                ref[j, rows, :] = v
                total, square = total + v, square + v * v
            sums[0, rows, :] = total
            sums[1, rows, :] = square

    sub = lax.broadcasted_iota(jnp.int32, (8, SPAN), 0)
    halo_rows = ((sub < 3) & (band < bands - 1)) | ((sub >= 5) & (band > 0))

    def wait_halo():
        @pl.when(band > 0)
        def _():
            wait_for(3, recv_sem.at[4])

        @pl.when(band < bands - 1)
        def _():
            wait_for(3, recv_sem.at[5])


    inner = (lax.broadcasted_iota(jnp.int32, (128, 128), 1) + jnp.where(two, 128, 0)) >= lax.broadcasted_iota(jnp.int32, (128, 128), 0)
    upper = lax.broadcasted_iota(jnp.int32, (128, 128), 1) >= lax.broadcasted_iota(jnp.int32, (128, 128), 0)

    def operands(trio):
        wraps = len(trio) == 3

        def box(sums, i, cols):
            h = joined(sums, trio, i)
            near = h[0:8]
            for k in range(1, 7):
                near = near + h[k:k + 8]
            if not wraps:
                return near
            far = h[8:16]
            for k in range(1, 7):
                far = far + h[8 + k:16 + k]
            return jnp.where(sub[:, :cols] >= 5, far, near)

        def stats(sums, cols):
            total = box(sums, 0, cols)
            mean = total * (1.0 / 49.0)
            spread = jnp.maximum(box(sums, 1, cols) * (1.0 / 49.0) - mean * mean, 0.01)
            return total, mean, lax.rsqrt(spread)

        total_l, _, scale_l = stats(lsum, 256)
        _, mean_r, scale_r = stats(rsum, 512)
        a, b = split3(-total_l), split3(mean_r)
        rt = jnp.concatenate([joined(rj, trio, j) for j in range(7)] + [b[q] for _, q in PAIRS], 0).astype(BF16)
        lt = jnp.concatenate([joined(lj, trio, j) for j in range(7)] + [a[p] for p, _ in PAIRS], 0).T.astype(BF16)
        return 8 * len(trio), lt, rt, scale_l * (1.0 / 49.0), scale_r

    def block(step, taps, lt, rt, scale_l, scale_r):
        lane = lax.broadcasted_iota(jnp.int32, (1, lt.shape[1]), 1)
        place = jnp.where(lane < 7 * taps, lane % taps, 100 + (lane - 7 * taps) % 8)
        for k in range(8):
            first = k + (8 if taps == 24 and k >= 5 else 0)
            keep = ((place >= first) & (place <= first + 6)) | (place == 100 + k)
            g = jnp.dot(lt * keep.astype(F32).astype(BF16), rt, preferred_element_type=F32)
            for half in range(2):
                rows = slice(128 * half, 128 * half + 128)
                part = [slice(128 * (half + i), 128 * (half + i + 1)) for i in range(3)]
                s = [g[rows, c] * scale_r[k:k + 1, c] for c in part]
                v = jnp.maximum(jnp.where(inner, s[1], s[2]), jnp.where(upper, jnp.where(two, s[0], s[1]), s[2]))
                v = v.T
                top = v[0:8]
                for q in range(8, 128, 8):
                    top = jnp.maximum(top, v[q:q + 8])
                tops[8 * step + k, :, rows] = top

    wait_for(8, recv_sem.at[0])
    prepare(0)
    wait_for(8, recv_sem.at[1])
    prepare(1)
    wait_for(8, recv_sem.at[2])
    wait_for(8, recv_sem.at[3])
    prepare(2)
    prepare(3)
    parts = [operands((0, 1))]
    parts.append(operands((1, 2)))
    parts.append(operands((2, 3)))
    block(0, *parts[0])
    block(1, *parts[1])
    wait_halo()
    prepare(4, halo_rows)
    parts.append(operands((3, 4, 0)))
    block(2, *parts[2])
    block(3, *parts[3])
    best = jnp.max(tops[...], axis=1) * jnp.concatenate([p[3] for p in parts], 0)
    best_ref[...] = pltpu.roll(best, 3, 0)

    wait_for(tiles - 1, send_sem.at[0])

    @pl.when(crosses)
    def _():
        wait_for(tiles, send_sem.at[1])


def solution(mesh):
    def on_device(left_image, right_image, ranges):
        arrays = [pltpu.with_memory_space_constraint(x, pltpu.HBM) for x in (ranges.T, left_image, right_image)]
        best = pl.pallas_call(
            kernel,
            out_shape=jax.ShapeDtypeStruct((32, 256), F32),
            in_specs=[pl.BlockSpec(memory_space=pltpu.HBM)] * 3,
            out_specs=pl.BlockSpec(memory_space=pltpu.VMEM),
            scratch_shapes=[
                pltpu.SMEM((2, 32), jnp.int32),
                pltpu.VMEM(left_image.shape, BF16),
                pltpu.VMEM(right_image.shape, BF16),
                pltpu.VMEM((2, left_image.shape[1] + 2 * PAD), BF16),
                pltpu.VMEM((40, 2, SPAN), BF16),
                pltpu.VMEM((7, 40, 256), F32),
                pltpu.VMEM((7, 40, 512), F32),
                pltpu.VMEM((2, 40, 256), F32),
                pltpu.VMEM((2, 40, 512), F32),
                pltpu.VMEM((32, 8, 256), F32),
                pltpu.SemaphoreType.DMA((3,)),
                pltpu.SemaphoreType.DMA((2,)),
                pltpu.SemaphoreType.DMA((6,)),
                pltpu.SemaphoreType.REGULAR,
            ],
            name="match",
            compiler_params=pltpu.CompilerParams(collective_id=0, has_side_effects=True, vmem_limit_bytes=16 << 20),
        )(*arrays)
        return jnp.maximum(best, -2.0)

    return jax.shard_map(
        on_device,
        mesh=mesh,
        in_specs=(P(("rows", "cols"), None), P(("rows", "cols"), None), P()),
        out_specs=P("rows", "cols"),
        check_vma=False,
    )
```
